512 devices in a mesh: obs: 8 (over y, core), cell: 64 (over x, z).
Axes of the slice: x: 4, y: 4, z: 16, core: 2. Of those that a mesh axis runs over, the one named last changes fastest.
Arguments:
- station_xy: float32 [2, 32768], P(None, 'obs'), may hold values from 0 to 8
- station_alt: float32 [32768], P('obs'), may hold values from 0.02 to 0.06
- cell_xy: float32 [2, 262144], P(None, 'cell'), may hold values from 0 to 8
- cell_depth: float32 [262144], P('cell'), may hold values from 0.04 to 0.12
- members: float32 [262144, 128], P('cell', 'obs'), may hold values from -6 to 6
- targets: float32 [32768, 128], P('obs'), may hold values from -9 to 9
- noise_var: float32 [32768], P('obs'), may hold values from 0.1 to 10
Outputs:
- increment: float32 [262144, 128], P('cell', 'obs')
The draws below stay inside these ranges and needn't reach their ends.
All inputs are finite; a program needn't handle non-finite values.
Results may differ from the reference program's by a relative error of at most 0.0006.
Values sent between devices are 32-bit elements; how exact they have to be, the bound alone decides.
A program may use at most 64 MiB of HBM per device.

```python
import math
import jax
import jax.numpy as jnp
from jax import lax

MEMBERS = 128
STATIONS = 32768
CELLS = 262144


def level_of(key, extent, pieces, smallest, high):
    level = 1.0
    for axis_at, parts in pieces:
        heights = jax.random.uniform(jax.random.fold_in(jax.random.fold_in(key, 6), axis_at), (parts,), jnp.float32, smallest / len(pieces), high / len(pieces))
        level = level * jnp.repeat(jnp.exp(heights), extent[axis_at] // parts).reshape((-1,) + (1,) * (len(extent) - 1 - axis_at))
    return level


def bell_draw(rng, extent, deviation, bound, cuts=(), held_as=jnp.bfloat16):
    array = jax.random.normal(rng, extent, jnp.float32) * deviation
    if len(cuts) > 0:
        array = level_of(rng, extent, cuts, -0.22, 0.18) * array
    return jnp.clip(array, min=-bound, max=bound).astype(held_as)


def setup_inputs(seed: int = 0) -> dict:
    key_list = jax.random.split(jax.random.key(seed), 8)
    station_xy = jnp.clip(8.0 * jax.random.uniform(key_list[0], (2, STATIONS), jnp.float32) ** level_of(key_list[0], (2, STATIONS), ((1, 8),), -0.2, 0.2), 0.0, 8.0)
    station_alt = jnp.clip(0.02 + 0.04 * jax.random.uniform(key_list[1], (STATIONS,), jnp.float32) ** level_of(key_list[1], (STATIONS,), ((0, 8),), -0.2, 0.2), 0.02, 0.06)
    cell_xy = jnp.clip(8.0 * jax.random.uniform(key_list[2], (2, CELLS), jnp.float32) ** level_of(key_list[2], (2, CELLS), ((1, 64),), -0.2, 0.2), 0.0, 8.0)
    cell_depth = jnp.clip(0.04 + 0.08 * jax.random.uniform(key_list[3], (CELLS,), jnp.float32) ** level_of(key_list[3], (CELLS,), ((0, 64),), -0.2, 0.2), 0.04, 0.12)
    members = bell_draw(key_list[4], (CELLS, MEMBERS), 1.0, 6.0, ((0, 64), (1, 8)), jnp.float32)
    targets = bell_draw(key_list[5], (STATIONS, MEMBERS), 1.5, 9.0, ((0, 8),), jnp.float32)
    noise_var = jnp.clip(jnp.exp(math.log(10.0) - 4.6051702 * jax.random.uniform(key_list[6], (STATIONS,), jnp.float32) ** level_of(key_list[6], (STATIONS,), ((0, 8),), -0.2, 0.2)), 0.1, 10.0)
    return {"station_xy": station_xy, "station_alt": station_alt, "cell_xy": cell_xy, "cell_depth": cell_depth, "members": members, "targets": targets, "noise_var": noise_var}


def kernel_rows(pos_x, pos_y, height, cell_xy, cell_depth, strength):
    delta_x = pos_x[:, None] - cell_xy[0][None, :]
    delta_y = pos_y[:, None] - cell_xy[1][None, :]
    depth_sum = height[:, None] + cell_depth[None, :]
    radius_sq = delta_x * delta_x + delta_y * delta_y + depth_sum * depth_sum
    inverse = lax.rsqrt(radius_sq)
    return (strength * depth_sum * inverse * inverse * inverse).astype(jnp.bfloat16)

def reference(station_xy, station_alt, cell_xy, cell_depth, members, targets, noise_var):
    strength = 1.0 / math.sqrt(CELLS)
    member_low = members.astype(jnp.bfloat16)
    block_rows = math.gcd(128, STATIONS)
    block_count = STATIONS // block_rows
    pos_x = station_xy[0].reshape(block_count, block_rows)
    pos_y = station_xy[1].reshape(block_count, block_rows)
    height = station_alt.reshape(block_count, block_rows)

    def one_block(inputs):
        kernel = kernel_rows(inputs[0], inputs[1], inputs[2], cell_xy, cell_depth, strength)
        return jnp.dot(kernel.astype(jnp.float32), member_low.astype(jnp.float32), preferred_element_type=jnp.float32)
    predicted = lax.map(one_block, (pos_x, pos_y, height)).reshape(STATIONS, MEMBERS)
    pred_anom = predicted - lax.optimization_barrier(jnp.mean(predicted, axis=1, keepdims=True))
    innovation = targets - predicted
    weighted = pred_anom / noise_var[:, None]
    gram_matrix = (MEMBERS - 1.0) * jnp.eye(MEMBERS, dtype=jnp.float32) + jnp.dot(weighted.T, pred_anom, precision=lax.Precision.HIGHEST)
    cross = jnp.dot(weighted.T, innovation, precision=lax.Precision.HIGHEST)
    coeffs = jnp.linalg.solve(gram_matrix, cross)
    member_anom = members - lax.optimization_barrier(jnp.mean(members, axis=1, keepdims=True))
    return jnp.dot(member_anom, coeffs, precision=lax.Precision.HIGHEST)
```

```python
import functools
import math

import jax
import jax.numpy as jnp
from jax import lax
from jax.experimental import pallas as pl
from jax.experimental.pallas import tpu as pltpu
from jax.sharding import PartitionSpec as P

MESH = pl.DeviceIdType.MESH
LANES = 128
WIDE = 512


def dot32(a, b, dims):
    return lax.dot_general(
        a, b, (dims, ((), ())), precision=lax.Precision.HIGHEST, preferred_element_type=jnp.float32
    )


def sums_kernel(nx, ny, nz, xy, alt, cell_xy, cell_dep, own, targets, noise,
                gathered_out, gram_out, cross_out,
                full, low, part, ring_in, x_in, tgt, wide_noise, rows, quarter, obs_in, eighth, z_in, group, total,
                g_send, g_recv, r_send, r_recv, x_send, x_recv, a_send, a_recv, o_send, o_recv,
                z_send, z_recv, b_send, b_recv, c_send, c_recv, local):
    obs, cell = lax.axis_index("obs"), lax.axis_index("cell")
    y, core = obs // 2, lax.rem(obs, 2)
    x, z = cell // nz, lax.rem(cell, nz)
    no = 2 * ny
    mine, cells = own.shape
    width = full.shape[0]
    stations = part.shape[0]
    chunk = stations // nz
    half = chunk // 2
    final = chunk // nx

    def obs_of(yy, cc):
        return lax.rem(yy + 2 * ny, ny) * 2 + cc

    def cell_of(xx, zz):
        return lax.rem(xx + 2 * nx, nx) * nz + lax.rem(zz + 4 * nz, nz)

    barrier = pltpu.get_barrier_semaphore()
    peers = [{"obs": lax.rem(obs + o, no)} for o in range(1, no)]
    peers += [{"cell": cell_of(x + o, z)} for o in range(1, nx)]
    peers += [{"cell": cell_of(x, z + o)} for o in range(1, nz)]
    for peer in peers:
        pl.semaphore_signal(barrier, inc=1, device_id=peer, device_id_type=MESH)

    mine_rows = pl.ds(pl.multiple_of(obs * mine, mine), mine)
    get_own = pltpu.make_async_copy(own, full.at[mine_rows], local.at[0])
    get_own.start()
    first = pl.multiple_of(z * chunk + x * final, final)
    get_tgt = pltpu.make_async_copy(targets.at[pl.ds(first, final)], tgt, local.at[1])
    get_tgt.start()
    get_own.wait()
    pl.semaphore_wait(barrier, len(peers))

    cut = cells // 2
    left, right, whole = pl.ds(0, cut), pl.ds(cut, cut), pl.ds(0, cells)

    def push(block, cols, target, slot):
        at = pl.ds(pl.multiple_of(block * mine, mine), mine)
        return pltpu.make_async_remote_copy(
            src_ref=full.at[at, cols], dst_ref=full.at[at, cols],
            send_sem=g_send.at[slot], recv_sem=g_recv.at[slot],
            device_id={"obs": target}, device_id_type=MESH,
        )

    mate, up, down = obs_of(y, 1 - core), obs_of(y + 1, core), obs_of(y - 1, core)
    far = obs_of(y + 2, core)
    sends = [push(obs, whole, mate, 0), push(obs, whole, up, 1), push(obs, whole, down, 2)]
    for c in sends:
        c.start()
    push(down, whole, up, 1).wait_recv()
    more = [push(down, left, up, 3), push(down, whole, mate, 4)]
    for c in more:
        c.start()
    sends += more
    push(up, whole, down, 2).wait_recv()
    more = [push(up, right, down, 5), push(up, whole, mate, 6)]
    for c in more:
        c.start()
    sends += more
    push(far, left, up, 3).wait_recv()
    more = [push(far, left, mate, 7)]
    more[0].start()
    sends += more
    push(far, right, down, 5).wait_recv()
    more = [push(far, right, mate, 8)]
    more[0].start()
    sends += more
    for slot, block, cols in (
        (0, mate, whole), (4, obs_of(y - 1, 1 - core), whole), (6, obs_of(y + 1, 1 - core), whole),
        (7, obs_of(y + 2, 1 - core), left), (8, obs_of(y + 2, 1 - core), right),
    ):
        push(block, cols, mate, slot).wait_recv()
    for c in sends:
        c.wait_send()
    save = pltpu.make_async_copy(full, gathered_out, local.at[2])
    save.start()
    for j in range(0, cells, WIDE):
        low[:, j:j + WIDE] = full[:, j:j + WIDE].astype(jnp.bfloat16)

    def ring_rows(way, step):
        at = lax.rem(z - 1 - step + 2 * nz, nz) if way == 0 else lax.rem(z + 1 + step, nz)
        return pl.ds(pl.multiple_of(at * chunk + way * half, half), half)

    def ring_copy(way, step):
        return pltpu.make_async_remote_copy(
            src_ref=part.at[ring_rows(way, step)], dst_ref=ring_in.at[way, step],
            send_sem=r_send.at[way, step], recv_sem=r_recv.at[way, step],
            device_id={"cell": cell_of(x, z + 1 - 2 * way)}, device_id_type=MESH,
        )

    def column(ref, row, at):
        tile = jnp.broadcast_to(ref[row:row + 1, at], (half, half)).T
        return jnp.concatenate([tile] * (WIDE // LANES), axis=1)

    def compute(step):
        ats = [ring_rows(0, step), ring_rows(1, step)]
        pos_x = jnp.concatenate([column(xy, 0, at) for at in ats], axis=0)
        pos_y = jnp.concatenate([column(xy, 1, at) for at in ats], axis=0)
        height = jnp.concatenate([column(alt, 0, at) for at in ats], axis=0)
        acc = jnp.zeros((chunk, width), jnp.float32)
        for j in range(0, cells, WIDE):
            dx = pos_x - cell_xy[0:1, j:j + WIDE]
            dy = pos_y - cell_xy[1:2, j:j + WIDE]
            h = height + cell_dep[0:1, j:j + WIDE]
            inverse = lax.rsqrt(dx * dx + dy * dy + h * h)
            kernel = ((h * inverse) * (inverse * inverse)).astype(jnp.bfloat16)
            acc += lax.dot_general(
                kernel, low[:, j:j + WIDE], (((1,), (1,)), ((), ())), preferred_element_type=jnp.float32
            )
        part[ats[0], :] = acc[:half]
        part[ats[1], :] = acc[half:]

    def ring_step(step, carry):
        compute(step)

        @pl.when(step > 0)
        def _():
            for way in range(2):
                ring_copy(way, step - 1).wait_recv()
                at = ring_rows(way, step)
                part[at, :] = part[at, :] + ring_in[way, step - 1]

        @pl.when(step < nz - 1)
        def _():
            for way in range(2):
                ring_copy(way, step).start()

        return carry

    lax.fori_loop(0, nz, ring_step, 0)

    x_copies = []
    for o in range(1, nx):
        to = lax.rem(x + o, nx)
        x_copies.append(pltpu.make_async_remote_copy(
            src_ref=part.at[pl.ds(pl.multiple_of(z * chunk + to * final, final), final)],
            dst_ref=x_in.at[o - 1], send_sem=x_send.at[o - 1], recv_sem=x_recv.at[o - 1],
            device_id={"cell": cell_of(x + o, z)}, device_id_type=MESH,
        ))
        x_copies[-1].start()
    window = pl.ds(pl.multiple_of(z * chunk + (x // 2) * LANES, LANES), LANES)
    wide_noise[...] = jnp.broadcast_to(noise[0:1, window], (LANES, LANES)).T
    variance = wide_noise[pl.ds(pl.multiple_of(lax.rem(x, 2) * final, final), final), :]
    get_tgt.wait()
    for c in x_copies:
        c.wait_recv()
    predicted = part[pl.ds(first, final), :]
    for o in range(nx - 1):
        predicted = predicted + x_in[o]
    predicted = predicted * (1.0 / math.sqrt(cells * nx * nz))

    anomaly = predicted - jnp.mean(predicted, axis=1, keepdims=True)
    weighted = anomaly / variance
    rows[0:width, :] = dot32(anomaly, weighted, ((0,), (0,)))
    rows[width:, :] = dot32(tgt[...] - predicted, weighted, ((0,), (0,)))

    deep = rows.shape[0] // nx
    thin = deep // no
    copies = []
    for o in range(1, nx):
        to = lax.rem(x + o, nx)
        copies.append(pltpu.make_async_remote_copy(
            src_ref=rows.at[pl.ds(pl.multiple_of(to * deep, deep), deep)],
            dst_ref=quarter.at[o - 1], send_sem=a_send.at[o - 1], recv_sem=a_recv.at[o - 1],
            device_id={"cell": cell_of(x + o, z)}, device_id_type=MESH,
        ))
        copies[-1].start()
    for c in copies:
        c.wait_recv()
    my_deep = pl.ds(pl.multiple_of(x * deep, deep), deep)
    value = rows[my_deep, :]
    for o in range(nx - 1):
        value = value + quarter[o]
    group[...] = value
    stage = []
    for o in range(1, no):
        to = lax.rem(obs + o, no)
        stage.append(pltpu.make_async_remote_copy(
            src_ref=group.at[pl.ds(pl.multiple_of(to * thin, thin), thin)],
            dst_ref=obs_in.at[o - 1], send_sem=o_send.at[o - 1], recv_sem=o_recv.at[o - 1],
            device_id={"obs": to}, device_id_type=MESH,
        ))
        stage[-1].start()
    for c in stage:
        c.wait_recv()
    copies += stage
    my_thin = pl.ds(pl.multiple_of(obs * thin, thin), thin)
    value = group[my_thin, :]
    for o in range(no - 1):
        value = value + obs_in[o]
    eighth[...] = value
    stage = []
    for o in range(1, nz):
        stage.append(pltpu.make_async_remote_copy(
            src_ref=eighth, dst_ref=z_in.at[o - 1], send_sem=z_send.at[o - 1], recv_sem=z_recv.at[o - 1],
            device_id={"cell": cell_of(x, z + o)}, device_id_type=MESH,
        ))
        stage[-1].start()
    for c in stage:
        c.wait_recv()
    copies += stage
    for o in range(nz - 1):
        value = value + z_in[o]
    back = pl.ds(pl.multiple_of(x * deep + obs * thin, thin), thin)
    total[back, :] = value
    stage = []
    for o in range(1, no):
        stage.append(pltpu.make_async_remote_copy(
            src_ref=total.at[back], dst_ref=total.at[back], send_sem=b_send.at[o - 1], recv_sem=b_recv.at[o - 1],
            device_id={"obs": lax.rem(obs + o, no)}, device_id_type=MESH,
        ))
        stage[-1].start()
    for o in range(1, no):
        at = pl.ds(pl.multiple_of(x * deep + lax.rem(obs + no - o, no) * thin, thin), thin)
        pltpu.make_async_remote_copy(
            src_ref=total.at[at], dst_ref=total.at[at], send_sem=b_send.at[o - 1], recv_sem=b_recv.at[o - 1],
            device_id={"obs": lax.rem(obs + o, no)}, device_id_type=MESH,
        ).wait_recv()
    copies += stage
    stage = []
    for o in range(1, nx):
        stage.append(pltpu.make_async_remote_copy(
            src_ref=total.at[my_deep], dst_ref=total.at[my_deep], send_sem=c_send.at[o - 1],
            recv_sem=c_recv.at[o - 1], device_id={"cell": cell_of(x + o, z)}, device_id_type=MESH,
        ))
        stage[-1].start()
    for o in range(1, nx):
        at = pl.ds(pl.multiple_of(lax.rem(x + nx - o, nx) * deep, deep), deep)
        pltpu.make_async_remote_copy(
            src_ref=total.at[at], dst_ref=total.at[at], send_sem=c_send.at[o - 1],
            recv_sem=c_recv.at[o - 1], device_id={"cell": cell_of(x + o, z)}, device_id_type=MESH,
        ).wait_recv()
    copies += stage
    gram_out[...] = total[0:width, :]
    cross_out[...] = total[pl.ds(pl.multiple_of(width + obs * mine, mine), mine), :]

    for c in x_copies + copies:
        c.wait_send()

    def drain(step, carry):
        for way in range(2):
            ring_copy(way, step).wait_send()
        return carry

    lax.fori_loop(0, nz - 1, drain, 0)
    save.wait()


def per_device(nx, ny, nz, station_xy, station_alt, cell_xy, cell_depth, members, targets, noise_var):
    own = members.T
    mine, cells = own.shape
    no = 2 * ny
    width = mine * no
    stations = station_alt.shape[0]
    chunk = stations // nz
    half, final = chunk // 2, chunk // nx
    deep = 2 * width // nx
    thin = deep // no
    f32 = jnp.float32
    vmem = pl.BlockSpec(memory_space=pltpu.VMEM)
    anyw = pl.BlockSpec(memory_space=pl.ANY)
    dma = pltpu.SemaphoreType.DMA
    gathered, gram, cross = pl.pallas_call(
        functools.partial(sums_kernel, nx, ny, nz),
        out_shape=(
            jax.ShapeDtypeStruct((width, cells), f32),
            jax.ShapeDtypeStruct((width, width), f32),
            jax.ShapeDtypeStruct((mine, width), f32),
        ),
        in_specs=[vmem, vmem, vmem, vmem, anyw, anyw, vmem],
        out_specs=(anyw, vmem, vmem),
        scratch_shapes=[
            pltpu.VMEM((width, cells), f32),
            pltpu.VMEM((width, cells), jnp.bfloat16),
            pltpu.VMEM((stations, width), f32),
            pltpu.VMEM((2, nz - 1, half, width), f32),
            pltpu.VMEM((nx - 1, final, width), f32),
            pltpu.VMEM((final, width), f32),
            pltpu.VMEM((LANES, LANES), f32),
            pltpu.VMEM((2 * width, width), f32),
            pltpu.VMEM((nx - 1, deep, width), f32),
            pltpu.VMEM((no - 1, thin, width), f32),
            pltpu.VMEM((thin, width), f32),
            pltpu.VMEM((nz - 1, thin, width), f32),
            pltpu.VMEM((deep, width), f32),
            pltpu.VMEM((2 * width, width), f32),
            dma((9,)), dma((9,)),
            dma((2, nz - 1)), dma((2, nz - 1)),
            dma((nx - 1,)), dma((nx - 1,)),
            dma((nx - 1,)), dma((nx - 1,)),
            dma((no - 1,)), dma((no - 1,)),
            dma((nz - 1,)), dma((nz - 1,)),
            dma((no - 1,)), dma((no - 1,)),
            dma((nx - 1,)), dma((nx - 1,)),
            dma((3,)),
        ],
        compiler_params=pltpu.CompilerParams(
            collective_id=0, has_side_effects=True, vmem_limit_bytes=48 * 2**20
        ),
    )(station_xy, station_alt[None], cell_xy, cell_depth[None], own, targets, noise_var[None])
    matrix = gram + (width - 1.0) * jnp.eye(width, dtype=f32)
    factor = jnp.linalg.cholesky(matrix)
    interim = lax.linalg.triangular_solve(factor, cross.T, left_side=True, lower=True)
    coeffs = lax.linalg.triangular_solve(factor, interim, left_side=True, lower=True, transpose_a=True)
    coeffs = coeffs - jnp.mean(coeffs, axis=0, keepdims=True)
    return jnp.dot(gathered.T, coeffs, precision=lax.Precision.HIGHEST)


def solution(mesh):
    nz = 16
    nx = mesh.shape["cell"] // nz
    ny = mesh.shape["obs"] // 2
    placed = (
        P(None, "obs"),
        P("obs"),
        P(None, "cell"),
        P("cell"),
        P("cell", "obs"),
        P("obs", None),
        P("obs"),
    )
    return jax.shard_map(
        functools.partial(per_device, nx, ny, nz),
        mesh=mesh, in_specs=placed, out_specs=P("cell", "obs"), check_vma=False,
    )
```

```python
import functools
import math

import jax
import jax.numpy as jnp
from jax import lax
from jax.experimental import pallas as pl
from jax.experimental.pallas import tpu as pltpu
from jax.sharding import PartitionSpec as P

MESH = pl.DeviceIdType.MESH
SUB = 8
LANES = 128
WIDE = 512


def dot32(a, b, dims):
    return lax.dot_general(
        a, b, (dims, ((), ())), precision=lax.Precision.HIGHEST, preferred_element_type=jnp.float32
    )


def sums_kernel(nx, ny, nz, xy_in, alt_in, cell_xy_in, cell_dep_in, own, targets, noise_in,
                gathered_out, gram_out, cross_out,
                xy, alt, cell_xy, cell_dep, noise,
                full, low, part, ring_in, x_in, tgt, wide_noise, rows, plane_in, eighth, z_in, total,
                g_send, g_recv, r_send, r_recv, x_send, x_recv, a_send, a_recv,
                z_send, z_recv, b_send, b_recv, local):
    obs, cell = lax.axis_index("obs"), lax.axis_index("cell")
    y, core = obs // 2, lax.rem(obs, 2)
    x, z = cell // nz, lax.rem(cell, nz)
    no = 2 * ny
    mine, cells = own.shape
    width = full.shape[0]
    stations = part.shape[0]
    chunk = stations // nz
    half = chunk // 2
    final = chunk // nx

    def obs_of(yy, cc):
        return lax.rem(yy + 2 * ny, ny) * 2 + cc

    def cell_of(xx, zz):
        return lax.rem(xx + 2 * nx, nx) * nz + lax.rem(zz + 4 * nz, nz)

    barrier = pltpu.get_barrier_semaphore()
    peers = [{"obs": o} for o in (obs_of(y, 1 - core), obs_of(y + 1, core), obs_of(y - 1, core))]
    peers += [{"cell": cell_of(x, z + 1)}, {"cell": cell_of(x, z - 1)}]
    peers += [{"cell": cell_of(x + o, z)} for o in range(1, nx)]
    for peer in peers:
        pl.semaphore_signal(barrier, inc=1, device_id=peer, device_id_type=MESH)

    mine_rows = pl.ds(pl.multiple_of(obs * mine, mine), mine)
    first = pl.multiple_of(z * chunk + x * final, final)
    loads = [
        pltpu.make_async_copy(src, dst, local.at[i]) for i, (src, dst) in enumerate((
            (own, full.at[mine_rows]), (xy_in, xy), (alt_in, alt), (cell_xy_in, cell_xy),
            (cell_dep_in, cell_dep), (noise_in, noise), (targets.at[pl.ds(first, final)], tgt),
        ))
    ]
    for c in loads:
        c.start()
    loads[0].wait()
    pl.semaphore_wait(barrier, len(peers))

    cut = cells // 2
    left, right, whole = pl.ds(0, cut), pl.ds(cut, cut), pl.ds(0, cells)

    def push(block, cols, target, slot):
        at = pl.ds(pl.multiple_of(block * mine, mine), mine)
        return pltpu.make_async_remote_copy(
            src_ref=full.at[at, cols], dst_ref=full.at[at, cols],
            send_sem=g_send.at[slot], recv_sem=g_recv.at[slot],
            device_id={"obs": target}, device_id_type=MESH,
        )

    mate, up, down = obs_of(y, 1 - core), obs_of(y + 1, core), obs_of(y - 1, core)
    far = obs_of(y + 2, core)
    sends = [push(obs, whole, mate, 0), push(obs, whole, up, 1), push(obs, whole, down, 2)]
    for c in sends:
        c.start()
    push(down, whole, up, 1).wait_recv()
    more = [push(down, left, up, 3), push(down, whole, mate, 4)]
    for c in more:
        c.start()
    sends += more
    push(up, whole, down, 2).wait_recv()
    more = [push(up, right, down, 5), push(up, whole, mate, 6)]
    for c in more:
        c.start()
    sends += more
    push(far, left, up, 3).wait_recv()
    more = [push(far, left, mate, 7)]
    more[0].start()
    sends += more
    push(far, right, down, 5).wait_recv()
    more = [push(far, right, mate, 8)]
    more[0].start()
    sends += more
    for slot, block, cols in (
        (0, mate, whole), (4, obs_of(y - 1, 1 - core), whole), (6, obs_of(y + 1, 1 - core), whole),
        (7, obs_of(y + 2, 1 - core), left), (8, obs_of(y + 2, 1 - core), right),
    ):
        push(block, cols, mate, slot).wait_recv()
    for c in sends:
        c.wait_send()
    save = pltpu.make_async_copy(full, gathered_out, local.at[7])
    save.start()
    for j in range(0, cells, WIDE):
        low[:, j:j + WIDE] = full[:, j:j + WIDE].astype(jnp.bfloat16)

    for c in loads[1:]:
        c.wait()

    def ring_rows(way, step):
        hop = step // 2
        at = lax.rem(z + nz // 2 - hop + nz, nz) if way == 0 else lax.rem(z + nz // 2 + 1 + hop, nz)
        return pl.ds(pl.multiple_of(at * chunk + lax.rem(step, 2) * half, half), half)

    def ring_copy(way, step):
        return pltpu.make_async_remote_copy(
            src_ref=part.at[ring_rows(way, step)], dst_ref=ring_in.at[way, step],
            send_sem=r_send.at[way, step], recv_sem=r_recv.at[way, step],
            device_id={"cell": cell_of(x, z + 1 - 2 * way)}, device_id_type=MESH,
        )

    def column(ref, row, at):
        tile = jnp.broadcast_to(ref[row:row + 1, at], (half, half)).T
        return jnp.concatenate([tile] * (WIDE // LANES), axis=1)

    def compute(step):
        ats = [ring_rows(0, step), ring_rows(1, step)]
        pos_x = jnp.concatenate([column(xy, 0, at) for at in ats], axis=0)
        pos_y = jnp.concatenate([column(xy, 1, at) for at in ats], axis=0)
        height = jnp.concatenate([column(alt, 0, at) for at in ats], axis=0)
        acc = jnp.zeros((chunk, width), jnp.float32)
        for j in range(0, cells, WIDE):
            dx = pos_x - cell_xy[0:1, j:j + WIDE]
            dy = pos_y - cell_xy[1:2, j:j + WIDE]
            h = height + cell_dep[0:1, j:j + WIDE]
            inverse = lax.rsqrt(dx * dx + dy * dy + h * h)
            kernel = ((h * inverse) * (inverse * inverse)).astype(jnp.bfloat16)
            acc += lax.dot_general(
                kernel, low[:, j:j + WIDE], (((1,), (1,)), ((), ())), preferred_element_type=jnp.float32
            )
        part[ats[0], :] = acc[:half]
        part[ats[1], :] = acc[half:]

    def ring_step(step, carry):
        compute(step)

        @pl.when(step > 1)
        def _():
            for way in range(2):
                ring_copy(way, step - 2).wait_recv()
                at = ring_rows(way, step)
                part[at, :] = part[at, :] + ring_in[way, step - 2]

        ring_copy(0, step).start()

        @pl.when(step < nz - 2)
        def _():
            ring_copy(1, step).start()

        return carry

    lax.fori_loop(0, nz, ring_step, 0)
    for step in (nz - 2, nz - 1):
        ring_copy(0, step).wait_recv()
        at = ring_rows(1, step)
        part[at, :] = part[at, :] + ring_in[0, step]

    x_copies = []
    for o in range(1, nx):
        to = lax.rem(x + o, nx)
        x_copies.append(pltpu.make_async_remote_copy(
            src_ref=part.at[pl.ds(pl.multiple_of(z * chunk + to * final, final), final)],
            dst_ref=x_in.at[o - 1], send_sem=x_send.at[o - 1], recv_sem=x_recv.at[o - 1],
            device_id={"cell": cell_of(x + o, z)}, device_id_type=MESH,
        ))
        x_copies[-1].start()
    window = pl.ds(pl.multiple_of(z * chunk + (x // 2) * LANES, LANES), LANES)
    wide_noise[...] = jnp.broadcast_to(noise[0:1, window], (LANES, LANES)).T
    variance = wide_noise[pl.ds(pl.multiple_of(lax.rem(x, 2) * final, final), final), :]
    for c in x_copies:
        c.wait_recv()
    predicted = part[pl.ds(first, final), :]
    for o in range(nx - 1):
        predicted = predicted + x_in[o]
    predicted = predicted * (1.0 / math.sqrt(cells * nx * nz))

    anomaly = predicted - jnp.mean(predicted, axis=1, keepdims=True)
    weighted = anomaly / variance
    rows[0:width, :] = dot32(anomaly, weighted, ((0,), (0,)))
    rows[width:, :] = dot32(tgt[...] - predicted, weighted, ((0,), (0,)))

    thin = rows.shape[0] // (nx * no)
    here = x * no + obs

    def spot(piece):
        return pl.ds(pl.multiple_of(piece * thin, thin), thin)

    def other(o):
        xx, oo = lax.rem(x + o // no, nx), lax.rem(obs + lax.rem(o, no), no)
        return xx * no + oo, {"cell": xx * nz + z, "obs": oo}

    def scatter(o):
        piece, device = other(o)
        return pltpu.make_async_remote_copy(
            src_ref=rows.at[spot(piece)], dst_ref=plane_in.at[o - 1],
            send_sem=a_send.at[o - 1], recv_sem=a_recv.at[o - 1], device_id=device, device_id_type=MESH,
        )

    def along(o):
        return pltpu.make_async_remote_copy(
            src_ref=eighth, dst_ref=z_in.at[o - 1], send_sem=z_send.at[o - 1], recv_sem=z_recv.at[o - 1],
            device_id={"cell": cell_of(x, z + o)}, device_id_type=MESH,
        )

    def gather(o):
        return pltpu.make_async_remote_copy(
            src_ref=total.at[spot(here)], dst_ref=total.at[spot(here)],
            send_sem=b_send.at[o - 1], recv_sem=b_recv.at[o - 1], device_id=other(o)[1], device_id_type=MESH,
        )

    def arrived(o):
        xx, oo = lax.rem(x + nx - o // no, nx), lax.rem(obs + no - lax.rem(o, no), no)
        at = spot(xx * no + oo)
        return pltpu.make_async_remote_copy(
            src_ref=total.at[at], dst_ref=total.at[at],
            send_sem=b_send.at[o - 1], recv_sem=b_recv.at[o - 1], device_id=other(o)[1], device_id_type=MESH,
        )

    def each(count, action):
        lax.fori_loop(1, count, lambda o, carry: (action(o), carry)[1], 0)

    spread = nx * no
    each(spread, lambda o: scatter(o).start())
    each(spread, lambda o: scatter(o).wait_recv())
    eighth[...] = rows[spot(here), :] + jnp.sum(plane_in[...], axis=0)
    each(nz, lambda o: along(o).start())
    each(nz, lambda o: along(o).wait_recv())
    total[spot(here), :] = eighth[...] + jnp.sum(z_in[...], axis=0)
    each(spread, lambda o: gather(o).start())
    each(spread, lambda o: arrived(o).wait_recv())
    gram_out[...] = total[0:width, :]
    cross_out[...] = total[pl.ds(pl.multiple_of(width + obs * mine, mine), mine), :]

    for c in x_copies:
        c.wait_send()
    each(spread, lambda o: scatter(o).wait_send())
    each(nz, lambda o: along(o).wait_send())
    each(spread, lambda o: gather(o).wait_send())

    def drain(step, carry):
        for way in range(2):
            ring_copy(way, step).wait_send()
        return carry

    lax.fori_loop(0, nz - 2, drain, 0)
    for step in (nz - 2, nz - 1):
        ring_copy(0, step).wait_send()
    save.wait()


def pair_inverse(a, b, d):
    scale = 1.0 / (a * d - b * b)
    return d * scale, -b * scale, a * scale


def quad_inverse(d):
    p0, p1, p2 = pair_inverse(d[0][0], d[1][0], d[1][1])
    q = [[d[2][0], d[3][0]], [d[2][1], d[3][1]]]
    u = [[p0 * q[0][j] + p1 * q[1][j] for j in range(2)], [p1 * q[0][j] + p2 * q[1][j] for j in range(2)]]
    s = [[d[2 + i][2 + j] - (q[0][i] * u[0][j] + q[1][i] * u[1][j]) for j in range(i + 1)] for i in range(2)]
    s0, s1, s2 = pair_inverse(s[0][0], s[1][0], s[1][1])
    v = [[u[i][0] * s0 + u[i][1] * s1, u[i][0] * s1 + u[i][1] * s2] for i in range(2)]
    top = [[p0 + v[0][0] * u[0][0] + v[0][1] * u[0][1]],
           [p1 + v[1][0] * u[0][0] + v[1][1] * u[0][1], p2 + v[1][0] * u[1][0] + v[1][1] * u[1][1]]]
    return [
        [top[0][0], top[1][0], -v[0][0], -v[0][1]],
        [top[1][0], top[1][1], -v[1][0], -v[1][1]],
        [-v[0][0], -v[1][0], s0, s1],
        [-v[0][1], -v[1][1], s1, s2],
    ]


def solve_kernel(gram, cross, members, out, full, high, low, sem):
    width, cells = full.shape
    fetch = pltpu.make_async_copy(members, full, sem.at[0])
    fetch.start()
    lane = lax.broadcasted_iota(jnp.int32, (SUB, LANES), 1)
    row = lax.broadcasted_iota(jnp.int32, (SUB, LANES), 0)
    tiles = [
        gram[i:i + SUB, :] + jnp.where(row + i == lane, width - 1.0, 0.0) for i in range(0, width, SUB)
    ]
    tiles += [cross[i:i + SUB, :] for i in range(0, cross.shape[0], SUB)]
    for k in range(0, width, 4):
        live = range((k + 4) // SUB, len(tiles))
        home, base = k // SUB, k % SUB
        pivot = tiles[home]

        def spread(tile, at):
            return jnp.broadcast_to(tile[:, at:at + 1], (SUB, LANES))

        def level(tile, at):
            return jnp.broadcast_to(tile[at:at + 1, :], (SUB, LANES))

        pivot_cols = [spread(pivot, k + j) for j in range(4)]
        block = [[level(pivot_cols[j], base + i) for j in range(i + 1)] for i in range(4)]
        inv = quad_inverse(block)
        steps = [level(pivot, base + i) for i in range(4)]
        moved = []
        for i in range(4):
            t = (inv[i][0] * steps[0] + inv[i][1] * steps[1]) + (inv[i][2] * steps[2] + inv[i][3] * steps[3])
            for m in range(4):
                t = jnp.where(lane == k + m, -inv[i][m], t)
            moved.append(t)
        for n in live:
            cols = pivot_cols if n == home else [spread(tiles[n], k + j) for j in range(4)]
            kept = jnp.where((lane >= k) & (lane < k + 4), 0.0, tiles[n])
            tiles[n] = kept - ((cols[0] * moved[0] + cols[1] * moved[1]) + (cols[2] * moved[2] + cols[3] * moved[3]))
        if k == width // 2:
            fetch.wait()
            for j in range(0, cells, 512):
                value = full[:, j:j + 512]
                top = value.astype(jnp.bfloat16)
                high[:, j:j + 512] = top
                low[:, j:j + 512] = (value - top.astype(jnp.float32)).astype(jnp.bfloat16)
    weights = jnp.concatenate(tiles[width // SUB:], axis=0)
    weights = weights - jnp.mean(weights, axis=1, keepdims=True)
    upper = weights.astype(jnp.bfloat16)
    lower = (weights - upper.astype(jnp.float32)).astype(jnp.bfloat16)
    both = jnp.concatenate([upper, lower], axis=0)
    n = upper.shape[0]
    for j in range(0, cells, 512):
        main = jnp.dot(both, high[:, j:j + 512], preferred_element_type=jnp.float32)
        rest = jnp.dot(upper, low[:, j:j + 512], preferred_element_type=jnp.float32)
        out[:, j:j + 512] = main[:n] + (main[n:] + rest)


def increments(gram, cross, gathered):
    width, cells = gathered.shape
    vmem = pl.BlockSpec(memory_space=pltpu.VMEM)
    return pl.pallas_call(
        solve_kernel,
        out_shape=jax.ShapeDtypeStruct((cross.shape[0], cells), jnp.float32),
        in_specs=[vmem, vmem, pl.BlockSpec(memory_space=pl.ANY)],
        out_specs=vmem,
        scratch_shapes=[
            pltpu.VMEM((width, cells), jnp.float32),
            pltpu.VMEM((width, cells), jnp.bfloat16),
            pltpu.VMEM((width, cells), jnp.bfloat16),
            pltpu.SemaphoreType.DMA((1,)),
        ],
        compiler_params=pltpu.CompilerParams(vmem_limit_bytes=24 * 2**20),
    )(gram, cross, gathered)


def per_device(nx, ny, nz, station_xy, station_alt, cell_xy, cell_depth, members, targets, noise_var):
    own = members.T
    mine, cells = own.shape
    no = 2 * ny
    width = mine * no
    stations = station_alt.shape[0]
    chunk = stations // nz
    half, final = chunk // 2, chunk // nx
    thin = 2 * width // (nx * no)
    f32 = jnp.float32
    vmem = pl.BlockSpec(memory_space=pltpu.VMEM)
    anyw = pl.BlockSpec(memory_space=pl.ANY)
    dma = pltpu.SemaphoreType.DMA
    gathered, gram, cross = pl.pallas_call(
        functools.partial(sums_kernel, nx, ny, nz),
        out_shape=(
            jax.ShapeDtypeStruct((width, cells), f32),
            jax.ShapeDtypeStruct((width, width), f32),
            jax.ShapeDtypeStruct((mine, width), f32),
        ),
        in_specs=[anyw] * 7,
        out_specs=(anyw, vmem, vmem),
        scratch_shapes=[
            pltpu.VMEM((2, stations), f32),
            pltpu.VMEM((1, stations), f32),
            pltpu.VMEM((2, cells), f32),
            pltpu.VMEM((1, cells), f32),
            pltpu.VMEM((1, stations), f32),
            pltpu.VMEM((width, cells), f32),
            pltpu.VMEM((width, cells), jnp.bfloat16),
            pltpu.VMEM((stations, width), f32),
            pltpu.VMEM((2, nz, half, width), f32),
            pltpu.VMEM((nx - 1, final, width), f32),
            pltpu.VMEM((final, width), f32),
            pltpu.VMEM((LANES, LANES), f32),
            pltpu.VMEM((2 * width, width), f32),
            pltpu.VMEM((nx * no - 1, thin, width), f32),
            pltpu.VMEM((thin, width), f32),
            pltpu.VMEM((nz - 1, thin, width), f32),
            pltpu.VMEM((2 * width, width), f32),
            dma((9,)), dma((9,)),
            dma((2, nz)), dma((2, nz)),
            dma((nx - 1,)), dma((nx - 1,)),
            dma((nx * no - 1,)), dma((nx * no - 1,)),
            dma((nz - 1,)), dma((nz - 1,)),
            dma((nx * no - 1,)), dma((nx * no - 1,)),
            dma((8,)),
        ],
        compiler_params=pltpu.CompilerParams(
            collective_id=0, has_side_effects=True, vmem_limit_bytes=48 * 2**20
        ),
    )(station_xy, station_alt[None], cell_xy, cell_depth[None], own, targets, noise_var[None])
    return increments(gram, cross, gathered).T


def solution(mesh):
    nz = 16
    nx = mesh.shape["cell"] // nz
    ny = mesh.shape["obs"] // 2
    placed = (
        P(None, "obs"),
        P("obs"),
        P(None, "cell"),
        P("cell"),
        P("cell", "obs"),
        P("obs", None),
        P("obs"),
    )
    return jax.shard_map(
        functools.partial(per_device, nx, ny, nz),
        mesh=mesh, in_specs=placed, out_specs=P("cell", "obs"), check_vma=False,
    )
```

```python
import functools
import math

import jax
import jax.numpy as jnp
from jax import lax
from jax.experimental import pallas as pl
from jax.experimental.pallas import tpu as pltpu
from jax.sharding import PartitionSpec as P

MESH = pl.DeviceIdType.MESH
SUB = 8
LANES = 128
WIDE = 512
AHEAD = (1, 3, 4, 5, 5)
CUTS = 1


def dot32(a, b, dims):
    return lax.dot_general(
        a, b, (dims, ((), ())), precision=lax.Precision.HIGHEST, preferred_element_type=jnp.float32
    )


def sums_kernel(nx, ny, nz, xy_in, alt_in, cell_xy_in, cell_dep_in, own, targets, noise_in,
                high_out, low_out, gram_out, cross_out,
                xy, alt, cell_xy, cell_dep, noise,
                full, low, rest, ahead, part, ring_in, x_in, tgt, wide_noise, rows, plane_in, eighth, z_in, total,
                g_send, g_recv, r_send, r_recv, x_send, x_recv, a_send, a_recv,
                z_send, z_recv, b_send, b_recv, local):
    obs, cell = lax.axis_index("obs"), lax.axis_index("cell")
    y, core = obs // 2, lax.rem(obs, 2)
    x, z = cell // nz, lax.rem(cell, nz)
    no = 2 * ny
    mine, cells = own.shape
    width = full.shape[0]
    stations = part.shape[0]
    chunk = stations // nz
    half = chunk // 2
    final = chunk // nx

    def obs_of(yy, cc):
        return lax.rem(yy + 2 * ny, ny) * 2 + cc

    def cell_of(xx, zz):
        return lax.rem(xx + 2 * nx, nx) * nz + lax.rem(zz + 4 * nz, nz)

    barrier = pltpu.get_barrier_semaphore()
    peers = [{"obs": o} for o in (obs_of(y, 1 - core), obs_of(y + 1, core), obs_of(y - 1, core))]
    peers += [{"cell": cell_of(x, z + 1)}, {"cell": cell_of(x, z - 1)}]
    peers += [{"cell": cell_of(x + o, z)} for o in range(1, nx)]
    for peer in peers:
        pl.semaphore_signal(barrier, inc=1, device_id=peer, device_id_type=MESH)

    mine_rows = pl.ds(pl.multiple_of(obs * mine, mine), mine)
    first = pl.multiple_of(z * chunk + x * final, final)
    loads = [
        pltpu.make_async_copy(src, dst, local.at[i]) for i, (src, dst) in enumerate((
            (own, full.at[mine_rows]), (xy_in, xy), (alt_in, alt), (cell_xy_in, cell_xy),
            (cell_dep_in, cell_dep), (noise_in, noise), (targets.at[pl.ds(first, final)], tgt),
        ))
    ]
    for c in loads:
        c.start()
    for c in loads:
        c.wait()

    def ring_rows(way, step):
        hop = step // 2
        at = lax.rem(z + nz // 2 - hop + nz, nz) if way == 0 else lax.rem(z + nz // 2 + 1 + hop, nz)
        return pl.ds(pl.multiple_of(at * chunk + lax.rem(step, 2) * half, half), half)

    def column(ref, row, at):
        tile = jnp.broadcast_to(ref[row:row + 1, at], (half, half)).T
        return jnp.concatenate([tile] * (WIDE // LANES), axis=1)

    def places(step):
        ats = [ring_rows(0, step), ring_rows(1, step)]
        return [jnp.concatenate([column(ref, row, at) for at in ats], axis=0) for ref, row in ((xy, 0), (xy, 1), (alt, 0))]

    def kernel_of(place, j):
        dx = place[0] - cell_xy[0:1, j:j + WIDE]
        dy = place[1] - cell_xy[1:2, j:j + WIDE]
        h = place[2] + cell_dep[0:1, j:j + WIDE]
        inverse = lax.rsqrt(dx * dx + dy * dy + h * h)
        return ((h * inverse) * (inverse * inverse)).astype(jnp.bfloat16)

    def times_members(kernel, j):
        return lax.dot_general(
            kernel, low[:, j:j + WIDE], (((1,), (1,)), ((), ())), preferred_element_type=jnp.float32
        )

    cut = cells // 2
    left, right, whole = pl.ds(0, cut), pl.ds(cut, cut), pl.ds(0, cells)

    def push(block, cols, target, slot):
        at = pl.ds(pl.multiple_of(block * mine, mine), mine)
        return pltpu.make_async_remote_copy(
            src_ref=full.at[at, cols], dst_ref=full.at[at, cols],
            send_sem=g_send.at[slot], recv_sem=g_recv.at[slot],
            device_id={"obs": target}, device_id_type=MESH,
        )

    mate, up, down = obs_of(y, 1 - core), obs_of(y + 1, core), obs_of(y - 1, core)
    far = obs_of(y + 2, core)
    own_up = [push(obs, left, up, 1), push(obs, right, up, 2)]
    own_down = [push(obs, right, down, 3), push(obs, left, down, 4)]
    pass_up, pass_down = push(down, left, up, 5), push(up, right, down, 6)
    to_mate = [
        push(obs, whole, mate, 0), push(down, whole, mate, 7), push(up, whole, mate, 8),
        push(far, left, mate, 9), push(far, right, mate, 10),
    ]
    sends = own_up + own_down + [pass_up, pass_down] + to_mate

    def build(step, carry):
        place = places(step)
        for j in range(0, cells, WIDE):
            ahead[step, :, j:j + WIDE] = kernel_of(place, j)

        @pl.when(step == AHEAD[0] - 1)
        def _():
            pl.semaphore_wait(barrier, len(peers))
            for c in (own_up[0], own_down[0], own_up[1], own_down[1], to_mate[0]):
                c.start()

        @pl.when(step == AHEAD[1] - 1)
        def _():
            push(down, left, up, 1).wait_recv()
            push(up, right, down, 3).wait_recv()
            pass_up.start()
            pass_down.start()

        @pl.when(step == AHEAD[2] - 1)
        def _():
            push(down, right, up, 2).wait_recv()
            push(up, left, down, 4).wait_recv()
            to_mate[1].start()
            to_mate[2].start()

        @pl.when(step == AHEAD[3] - 1)
        def _():
            push(far, left, up, 5).wait_recv()
            push(far, right, down, 6).wait_recv()
            to_mate[3].start()
            to_mate[4].start()

        return carry

    lax.fori_loop(0, AHEAD[-1], build, 0)
    for slot, block, cols in (
        (0, mate, whole), (7, obs_of(y - 1, 1 - core), whole), (8, obs_of(y + 1, 1 - core), whole),
        (9, obs_of(y + 2, 1 - core), left), (10, obs_of(y + 2, 1 - core), right),
    ):
        push(block, cols, mate, slot).wait_recv()
    for j in range(0, cells, WIDE):
        low[:, j:j + WIDE] = full[:, j:j + WIDE].astype(jnp.bfloat16)
    saves = [pltpu.make_async_copy(low, high_out, local.at[7]), pltpu.make_async_copy(rest, low_out, local.at[8])]
    saves[0].start()

    def ring_rows_of(way, step, piece):
        rows_at = ring_rows(way, step)
        return pl.ds(pl.multiple_of(rows_at.start + piece * (half // CUTS), half // CUTS), half // CUTS)

    def ring_copy(way, step, piece):
        return pltpu.make_async_remote_copy(
            src_ref=part.at[ring_rows_of(way, step, piece)],
            dst_ref=ring_in.at[way, step, pl.ds(piece * (half // CUTS), half // CUTS)],
            send_sem=r_send.at[way, step, piece], recv_sem=r_recv.at[way, step, piece],
            device_id={"cell": cell_of(x, z + 1 - 2 * way)}, device_id_type=MESH,
        )

    def take(way, step, target, piece):
        ring_copy(way, step, piece).wait_recv()
        at = ring_rows_of(target[0], target[1], piece)
        part[at, :] = part[at, :] + ring_in[way, step, pl.ds(piece * (half // CUTS), half // CUTS)]

    def ring_step(step, kernels):
        acc = jnp.zeros((chunk, width), jnp.float32)
        for j in range(0, cells, WIDE):
            acc += times_members(kernels(j), j)
        part[ring_rows(0, step), :] = acc[:half]
        part[ring_rows(1, step), :] = acc[half:]

        for piece in range(CUTS):
            for way in range(2):
                @pl.when(step > 1)
                def _():
                    take(way, step - 2, (way, step), piece)

                if way == 0:
                    ring_copy(0, step, piece).start()
                else:
                    @pl.when(step < nz - 2)
                    def _():
                        ring_copy(1, step, piece).start()

    def built_step(step, carry):
        ring_step(step, lambda j: ahead[step, :, j:j + WIDE])
        return carry

    def fresh_step(step, carry):
        place = places(step)
        ring_step(step, lambda j: kernel_of(place, j))
        return carry

    lax.fori_loop(0, AHEAD[-1], built_step, 0)
    lax.fori_loop(AHEAD[-1], nz, fresh_step, 0)
    for step in (nz - 2, nz - 1):
        for piece in range(CUTS):
            take(0, step, (1, step), piece)

    x_copies = []
    for o in sorted(range(1, nx), key=lambda o: abs(o - nx // 2)):
        to = lax.rem(x + o, nx)
        x_copies.append(pltpu.make_async_remote_copy(
            src_ref=part.at[pl.ds(pl.multiple_of(z * chunk + to * final, final), final)],
            dst_ref=x_in.at[o - 1], send_sem=x_send.at[o - 1], recv_sem=x_recv.at[o - 1],
            device_id={"cell": cell_of(x + o, z)}, device_id_type=MESH,
        ))
        x_copies[-1].start()
    window = pl.ds(pl.multiple_of(z * chunk + (x // 2) * LANES, LANES), LANES)
    wide_noise[...] = jnp.broadcast_to(noise[0:1, window], (LANES, LANES)).T
    variance = wide_noise[pl.ds(pl.multiple_of(lax.rem(x, 2) * final, final), final), :]
    for c in x_copies:
        c.wait_recv()
    predicted = part[pl.ds(first, final), :]
    for o in range(nx - 1):
        predicted = predicted + x_in[o]
    predicted = predicted * (1.0 / math.sqrt(cells * nx * nz))

    anomaly = predicted - jnp.mean(predicted, axis=1, keepdims=True)
    weighted = anomaly / variance
    rows[0:width, :] = dot32(anomaly, weighted, ((0,), (0,)))
    rows[width:, :] = dot32(tgt[...] - predicted, weighted, ((0,), (0,)))

    thin = rows.shape[0] // (nx * no)
    here = x * no + obs

    def spot(piece):
        return pl.ds(pl.multiple_of(piece * thin, thin), thin)

    def other(o):
        xx, oo = lax.rem(x + o // no, nx), lax.rem(obs + lax.rem(o, no), no)
        return xx * no + oo, {"cell": xx * nz + z, "obs": oo}

    def scatter(o):
        piece, device = other(o)
        return pltpu.make_async_remote_copy(
            src_ref=rows.at[spot(piece)], dst_ref=plane_in.at[o - 1],
            send_sem=a_send.at[o - 1], recv_sem=a_recv.at[o - 1], device_id=device, device_id_type=MESH,
        )

    def along(o):
        return pltpu.make_async_remote_copy(
            src_ref=eighth, dst_ref=z_in.at[o - 1], send_sem=z_send.at[o - 1], recv_sem=z_recv.at[o - 1],
            device_id={"cell": cell_of(x, z + o)}, device_id_type=MESH,
        )

    def gather(o):
        return pltpu.make_async_remote_copy(
            src_ref=total.at[spot(here)], dst_ref=total.at[spot(here)],
            send_sem=b_send.at[o - 1], recv_sem=b_recv.at[o - 1], device_id=other(o)[1], device_id_type=MESH,
        )

    def arrived(o):
        xx, oo = lax.rem(x + nx - o // no, nx), lax.rem(obs + no - lax.rem(o, no), no)
        at = spot(xx * no + oo)
        return pltpu.make_async_remote_copy(
            src_ref=total.at[at], dst_ref=total.at[at],
            send_sem=b_send.at[o - 1], recv_sem=b_recv.at[o - 1], device_id=other(o)[1], device_id_type=MESH,
        )

    def fan(i, middle):
        return middle + ((i + 1) // 2) * (1 - 2 * lax.rem(i, 2))

    def over_plane(action):
        def one(i, carry):
            action(fan(i // no, nx // 2) * no + fan(lax.rem(i, no), no // 2))
            return carry

        lax.fori_loop(0, nx * no - 1, one, 0)

    def over_z(action):
        def one(i, carry):
            action(fan(i, nz // 2))
            return carry

        lax.fori_loop(0, nz - 1, one, 0)

    over_plane(lambda o: scatter(o).start())
    for j in range(0, cells, WIDE):
        exact = full[:, j:j + WIDE]
        rest[:, j:j + WIDE] = (exact - low[:, j:j + WIDE].astype(jnp.float32)).astype(jnp.bfloat16)
    saves[1].start()
    over_plane(lambda o: scatter(o).wait_recv())
    eighth[...] = rows[spot(here), :] + jnp.sum(plane_in[...], axis=0)
    over_z(lambda o: along(o).start())
    for c in sends + x_copies:
        c.wait_send()

    def drain(step, carry):
        for piece in range(CUTS):
            ring_copy(0, step, piece).wait_send()

            @pl.when(step < nz - 2)
            def _():
                ring_copy(1, step, piece).wait_send()

        return carry

    lax.fori_loop(0, nz, drain, 0)
    over_plane(lambda o: scatter(o).wait_send())
    over_z(lambda o: along(o).wait_recv())
    total[spot(here), :] = eighth[...] + jnp.sum(z_in[...], axis=0)
    over_plane(lambda o: gather(o).start())
    over_z(lambda o: along(o).wait_send())
    for c in saves:
        c.wait()
    over_plane(lambda o: arrived(o).wait_recv())
    gram_out[...] = total[0:width, :]
    cross_out[...] = total[pl.ds(pl.multiple_of(width + obs * mine, mine), mine), :]
    over_plane(lambda o: gather(o).wait_send())


def pair_inverse(a, b, d):
    scale = 1.0 / (a * d - b * b)
    return d * scale, -b * scale, a * scale


def quad_inverse(d):
    p0, p1, p2 = pair_inverse(d[0][0], d[1][0], d[1][1])
    q = [[d[2][0], d[3][0]], [d[2][1], d[3][1]]]
    u = [[p0 * q[0][j] + p1 * q[1][j] for j in range(2)], [p1 * q[0][j] + p2 * q[1][j] for j in range(2)]]
    s = [[d[2 + i][2 + j] - (q[0][i] * u[0][j] + q[1][i] * u[1][j]) for j in range(i + 1)] for i in range(2)]
    s0, s1, s2 = pair_inverse(s[0][0], s[1][0], s[1][1])
    v = [[u[i][0] * s0 + u[i][1] * s1, u[i][0] * s1 + u[i][1] * s2] for i in range(2)]
    top = [[p0 + v[0][0] * u[0][0] + v[0][1] * u[0][1]],
           [p1 + v[1][0] * u[0][0] + v[1][1] * u[0][1], p2 + v[1][0] * u[1][0] + v[1][1] * u[1][1]]]
    return [
        [top[0][0], top[1][0], -v[0][0], -v[0][1]],
        [top[1][0], top[1][1], -v[1][0], -v[1][1]],
        [-v[0][0], -v[1][0], s0, s1],
        [-v[0][1], -v[1][1], s1, s2],
    ]


def solve_kernel(gram, cross, high_in, low_in, out, high, low, sem):
    width, cells = high.shape
    fetches = [pltpu.make_async_copy(high_in, high, sem.at[0]), pltpu.make_async_copy(low_in, low, sem.at[1])]
    for c in fetches:
        c.start()
    lane = lax.broadcasted_iota(jnp.int32, (SUB, LANES), 1)
    row = lax.broadcasted_iota(jnp.int32, (SUB, LANES), 0)
    tiles = [
        gram[i:i + SUB, :] + jnp.where(row + i == lane, width - 1.0, 0.0) for i in range(0, width, SUB)
    ]
    tiles += [cross[i:i + SUB, :] for i in range(0, cross.shape[0], SUB)]
    for k in range(0, width, 4):
        live = range((k + 4) // SUB, len(tiles))
        home, base = k // SUB, k % SUB
        pivot = tiles[home]

        def spread(tile, at):
            return jnp.broadcast_to(tile[:, at:at + 1], (SUB, LANES))

        def level(tile, at):
            return jnp.broadcast_to(tile[at:at + 1, :], (SUB, LANES))

        pivot_cols = [spread(pivot, k + j) for j in range(4)]
        block = [[level(pivot_cols[j], base + i) for j in range(i + 1)] for i in range(4)]
        inv = quad_inverse(block)
        steps = [level(pivot, base + i) for i in range(4)]
        moved = []
        for i in range(4):
            t = (inv[i][0] * steps[0] + inv[i][1] * steps[1]) + (inv[i][2] * steps[2] + inv[i][3] * steps[3])
            for m in range(4):
                t = jnp.where(lane == k + m, -inv[i][m], t)
            moved.append(t)
        for n in live:
            cols = pivot_cols if n == home else [spread(tiles[n], k + j) for j in range(4)]
            kept = jnp.where((lane >= k) & (lane < k + 4), 0.0, tiles[n])
            tiles[n] = kept - ((cols[0] * moved[0] + cols[1] * moved[1]) + (cols[2] * moved[2] + cols[3] * moved[3]))
    weights = jnp.concatenate(tiles[width // SUB:], axis=0)
    weights = weights - jnp.mean(weights, axis=1, keepdims=True)
    upper = weights.astype(jnp.bfloat16)
    lower = (weights - upper.astype(jnp.float32)).astype(jnp.bfloat16)
    both = jnp.concatenate([upper, lower], axis=0)
    for c in fetches:
        c.wait()
    n = upper.shape[0]
    for j in range(0, cells, 512):
        main = jnp.dot(both, high[:, j:j + 512], preferred_element_type=jnp.float32)
        rest = jnp.dot(upper, low[:, j:j + 512], preferred_element_type=jnp.float32)
        out[:, j:j + 512] = main[:n] + (main[n:] + rest)


def increments(gram, cross, high, low):
    width, cells = high.shape
    vmem = pl.BlockSpec(memory_space=pltpu.VMEM)
    return pl.pallas_call(
        solve_kernel,
        out_shape=jax.ShapeDtypeStruct((cross.shape[0], cells), jnp.float32),
        in_specs=[vmem, vmem, pl.BlockSpec(memory_space=pl.ANY), pl.BlockSpec(memory_space=pl.ANY)],
        out_specs=vmem,
        scratch_shapes=[
            pltpu.VMEM((width, cells), jnp.bfloat16),
            pltpu.VMEM((width, cells), jnp.bfloat16),
            pltpu.SemaphoreType.DMA((2,)),
        ],
        compiler_params=pltpu.CompilerParams(vmem_limit_bytes=64 * 2**20),
    )(gram, cross, high, low)


def per_device(nx, ny, nz, station_xy, station_alt, cell_xy, cell_depth, members, targets, noise_var):
    own = members.T
    mine, cells = own.shape
    no = 2 * ny
    width = mine * no
    stations = station_alt.shape[0]
    chunk = stations // nz
    half, final = chunk // 2, chunk // nx
    thin = 2 * width // (nx * no)
    f32 = jnp.float32
    vmem = pl.BlockSpec(memory_space=pltpu.VMEM)
    anyw = pl.BlockSpec(memory_space=pl.ANY)
    dma = pltpu.SemaphoreType.DMA
    high, low, gram, cross = pl.pallas_call(
        functools.partial(sums_kernel, nx, ny, nz),
        out_shape=(
            jax.ShapeDtypeStruct((width, cells), jnp.bfloat16),
            jax.ShapeDtypeStruct((width, cells), jnp.bfloat16),
            jax.ShapeDtypeStruct((width, width), f32),
            jax.ShapeDtypeStruct((mine, width), f32),
        ),
        in_specs=[pl.BlockSpec(memory_space=pltpu.HBM)] * 7,
        out_specs=(anyw, anyw, vmem, vmem),
        scratch_shapes=[
            pltpu.VMEM((2, stations), f32),
            pltpu.VMEM((1, stations), f32),
            pltpu.VMEM((2, cells), f32),
            pltpu.VMEM((1, cells), f32),
            pltpu.VMEM((1, stations), f32),
            pltpu.VMEM((width, cells), f32),
            pltpu.VMEM((width, cells), jnp.bfloat16),
            pltpu.VMEM((width, cells), jnp.bfloat16),
            pltpu.VMEM((AHEAD[-1], chunk, cells), jnp.bfloat16),
            pltpu.VMEM((stations, width), f32),
            pltpu.VMEM((2, nz, half, width), f32),
            pltpu.VMEM((nx - 1, final, width), f32),
            pltpu.VMEM((final, width), f32),
            pltpu.VMEM((LANES, LANES), f32),
            pltpu.VMEM((2 * width, width), f32),
            pltpu.VMEM((nx * no - 1, thin, width), f32),
            pltpu.VMEM((thin, width), f32),
            pltpu.VMEM((nz - 1, thin, width), f32),
            pltpu.VMEM((2 * width, width), f32),
            dma((11,)), dma((11,)),
            dma((2, nz, CUTS)), dma((2, nz, CUTS)),
            dma((nx - 1,)), dma((nx - 1,)),
            dma((nx * no - 1,)), dma((nx * no - 1,)),
            dma((nz - 1,)), dma((nz - 1,)),
            dma((nx * no - 1,)), dma((nx * no - 1,)),
            dma((9,)),
        ],
        compiler_params=pltpu.CompilerParams(
            collective_id=0, has_side_effects=True, vmem_limit_bytes=64 * 2**20
        ),
    )(station_xy, station_alt[None], cell_xy, cell_depth[None], own, targets, noise_var[None])
    return increments(gram, cross, high, low).T


def solution(mesh):
    nz = 16
    nx = mesh.shape["cell"] // nz
    ny = mesh.shape["obs"] // 2
    placed = (
        P(None, "obs"),
        P("obs"),
        P(None, "cell"),
        P("cell"),
        P("cell", "obs"),
        P("obs", None),
        P("obs"),
    )
    return jax.shard_map(
        functools.partial(per_device, nx, ny, nz),
        mesh=mesh, in_specs=placed, out_specs=P("cell", "obs"), check_vma=False,
    )
```

```python
import functools
import math

import jax
import jax.numpy as jnp
from jax import lax
from jax.experimental import pallas as pl
from jax.experimental.pallas import tpu as pltpu
from jax.sharding import PartitionSpec as P

MESH = pl.DeviceIdType.MESH
SUB = 8
LANES = 128
WIDE = 512
AHEAD = (2, 2, 2, 2)
PAIR = 2
CUTS = 1


def dot32(a, b, dims):
    return lax.dot_general(
        a, b, (dims, ((), ())), precision=lax.Precision.HIGHEST, preferred_element_type=jnp.float32
    )


def pair_inverse(a, b, d):
    scale = 1.0 / (a * d - b * b)
    return d * scale, -b * scale, a * scale


def quad_inverse(d):
    p0, p1, p2 = pair_inverse(d[0][0], d[1][0], d[1][1])
    q = [[d[2][0], d[3][0]], [d[2][1], d[3][1]]]
    u = [[p0 * q[0][j] + p1 * q[1][j] for j in range(2)], [p1 * q[0][j] + p2 * q[1][j] for j in range(2)]]
    s = [[d[2 + i][2 + j] - (q[0][i] * u[0][j] + q[1][i] * u[1][j]) for j in range(i + 1)] for i in range(2)]
    s0, s1, s2 = pair_inverse(s[0][0], s[1][0], s[1][1])
    v = [[u[i][0] * s0 + u[i][1] * s1, u[i][0] * s1 + u[i][1] * s2] for i in range(2)]
    top = [[p0 + v[0][0] * u[0][0] + v[0][1] * u[0][1]],
           [p1 + v[1][0] * u[0][0] + v[1][1] * u[0][1], p2 + v[1][0] * u[1][0] + v[1][1] * u[1][1]]]
    return [
        [top[0][0], top[1][0], -v[0][0], -v[0][1]],
        [top[1][0], top[1][1], -v[1][0], -v[1][1]],
        [-v[0][0], -v[1][0], s0, s1],
        [-v[0][1], -v[1][1], s1, s2],
    ]


def solve_rows(gram, cross):
    width = SUB * len(gram)
    lane = lax.broadcasted_iota(jnp.int32, (SUB, LANES), 1)
    row = lax.broadcasted_iota(jnp.int32, (SUB, LANES), 0)
    tiles = [
        gram[i // SUB] + jnp.where(row + i == lane, width - 1.0, 0.0) for i in range(0, width, SUB)
    ]
    tiles += [cross[i:i + SUB] for i in range(0, cross.shape[0], SUB)]
    for k in range(0, width, 4):
        live = range((k + 4) // SUB, len(tiles))
        home, base = k // SUB, k % SUB
        pivot = tiles[home]

        def spread(tile, at):
            return jnp.broadcast_to(tile[:, at:at + 1], (SUB, LANES))

        def level(tile, at):
            return jnp.broadcast_to(tile[at:at + 1, :], (SUB, LANES))

        pivot_cols = [spread(pivot, k + j) for j in range(4)]
        block = [[level(pivot_cols[j], base + i) for j in range(i + 1)] for i in range(4)]
        inv = quad_inverse(block)
        steps = [level(pivot, base + i) for i in range(4)]
        moved = []
        for i in range(4):
            t = (inv[i][0] * steps[0] + inv[i][1] * steps[1]) + (inv[i][2] * steps[2] + inv[i][3] * steps[3])
            for m in range(4):
                t = jnp.where(lane == k + m, -inv[i][m], t)
            moved.append(t)
        for n in live:
            cols = pivot_cols if n == home else [spread(tiles[n], k + j) for j in range(4)]
            kept = jnp.where((lane >= k) & (lane < k + 4), 0.0, tiles[n])
            tiles[n] = kept - ((cols[0] * moved[0] + cols[1] * moved[1]) + (cols[2] * moved[2] + cols[3] * moved[3]))
    return jnp.concatenate(tiles[width // SUB:], axis=0)


def sums_kernel(nx, ny, nz, xy_in, alt_in, cell_xy_in, cell_dep_in, own, targets, noise_in,
                out,
                xy, alt, cell_xy, cell_dep, noise,
                full, low, rest, ahead, part, ring_in, x_in, tgt, wide_noise, rows, plane_in, eighth, z_in, total,
                g_send, g_recv, r_send, r_recv, x_send, x_recv, a_send, a_recv,
                z_send, z_recv, b_send, b_recv, local):
    obs, cell = lax.axis_index("obs"), lax.axis_index("cell")
    y, core = obs // 2, lax.rem(obs, 2)
    x, z = cell // nz, lax.rem(cell, nz)
    no = 2 * ny
    mine, cells = own.shape
    width = full.shape[0]
    stations = part.shape[0]
    chunk = stations // nz
    half = chunk // 2
    final = chunk // nx

    def obs_of(yy, cc):
        return lax.rem(yy + 2 * ny, ny) * 2 + cc

    def cell_of(xx, zz):
        return lax.rem(xx + 2 * nx, nx) * nz + lax.rem(zz + 4 * nz, nz)

    barrier = pltpu.get_barrier_semaphore()
    peers = [{"obs": o} for o in (obs_of(y, 1 - core), obs_of(y + 1, core), obs_of(y - 1, core))]
    peers += [{"cell": cell_of(x, z + 1)}, {"cell": cell_of(x, z - 1)}]
    peers += [{"cell": cell_of(x + o, z)} for o in range(1, nx)]
    for peer in peers:
        pl.semaphore_signal(barrier, inc=1, device_id=peer, device_id_type=MESH)

    mine_rows = pl.ds(pl.multiple_of(obs * mine, mine), mine)
    first = pl.multiple_of(z * chunk + x * final, final)
    loads = [
        pltpu.make_async_copy(src, dst, local.at[i]) for i, (src, dst) in enumerate((
            (own, full.at[mine_rows]), (xy_in, xy), (alt_in, alt), (cell_xy_in, cell_xy),
            (cell_dep_in, cell_dep), (noise_in, noise), (targets.at[pl.ds(first, final)], tgt),
        ))
    ]
    for c in loads:
        c.start()
    def ring_rows(way, step):
        hop = step // 2
        at = lax.rem(z + nz + nz // 2 - hop + way * (1 + 2 * hop), nz)
        return pl.ds(pl.multiple_of(at * chunk + lax.rem(step, 2) * half, half), half)

    def column(ref, row, at):
        tile = jnp.broadcast_to(ref[row:row + 1, at], (half, half)).T
        return jnp.concatenate([tile] * (WIDE // LANES), axis=1)

    def places(step):
        return places_at([ring_rows(0, step), ring_rows(1, step)])

    def places_at(ats):
        return [jnp.concatenate([column(ref, row, at) for at in ats], axis=0) for ref, row in ((xy, 0), (xy, 1), (alt, 0))]

    def kernel_of(place, j):
        dx = place[0] - cell_xy[0:1, j:j + WIDE]
        dy = place[1] - cell_xy[1:2, j:j + WIDE]
        h = place[2] + cell_dep[0:1, j:j + WIDE]
        inverse = lax.rsqrt(dx * dx + dy * dy + h * h)
        return ((h * inverse) * (inverse * inverse)).astype(jnp.bfloat16)

    def times_members(kernel, j):
        return lax.dot_general(
            kernel, low[:, j:j + WIDE], (((1,), (1,)), ((), ())), preferred_element_type=jnp.float32
        )

    cut = cells // 2
    left, right, whole = pl.ds(0, cut), pl.ds(cut, cut), pl.ds(0, cells)

    def push(block, cols, target, slot):
        at = pl.ds(pl.multiple_of(block * mine, mine), mine)
        return pltpu.make_async_remote_copy(
            src_ref=full.at[at, cols], dst_ref=full.at[at, cols],
            send_sem=g_send.at[slot], recv_sem=g_recv.at[slot],
            device_id={"obs": target}, device_id_type=MESH,
        )

    mate, up, down = obs_of(y, 1 - core), obs_of(y + 1, core), obs_of(y - 1, core)
    far = obs_of(y + 2, core)
    def push_own(cols, target, slot):
        return pltpu.make_async_remote_copy(
            src_ref=own.at[:, cols], dst_ref=full.at[mine_rows, cols],
            send_sem=g_send.at[slot], recv_sem=g_recv.at[slot],
            device_id={"obs": target}, device_id_type=MESH,
        )

    own_up = [push_own(left, up, 1), push_own(right, up, 2)]
    own_down = [push_own(right, down, 3), push_own(left, down, 4)]
    pass_up, pass_down = push(down, left, up, 5), push(up, right, down, 6)
    to_mate = [
        push_own(whole, mate, 0), push(down, whole, mate, 7), push(up, whole, mate, 8),
        push(far, left, mate, 9), push(far, right, mate, 10),
    ]
    sends = own_up + own_down + [pass_up, pass_down] + to_mate

    pl.semaphore_wait(barrier, len(peers))
    for c in (own_up[0], own_down[0], own_up[1], own_down[1], to_mate[0]):
        c.start()
    for c in loads:
        c.wait()

    def build(step, carry):
        place = places(step)
        for j in range(0, cells, WIDE):
            ahead[step, :, j:j + WIDE] = kernel_of(place, j)

        @pl.when(step == AHEAD[0] - 1)
        def _():
            push(down, left, up, 1).wait_recv()
            push(up, right, down, 3).wait_recv()
            pass_up.start()
            pass_down.start()

        @pl.when(step == AHEAD[1] - 1)
        def _():
            push(down, right, up, 2).wait_recv()
            push(up, left, down, 4).wait_recv()
            to_mate[1].start()
            to_mate[2].start()

        @pl.when(step == AHEAD[2] - 1)
        def _():
            push(far, left, up, 5).wait_recv()
            push(far, right, down, 6).wait_recv()
            to_mate[3].start()
            to_mate[4].start()

        return carry

    lax.fori_loop(0, AHEAD[-1], build, 0)
    for slot, block, cols in (
        (0, mate, whole), (7, obs_of(y - 1, 1 - core), whole), (8, obs_of(y + 1, 1 - core), whole),
        (9, obs_of(y + 2, 1 - core), left), (10, obs_of(y + 2, 1 - core), right),
    ):
        push(block, cols, mate, slot).wait_recv()
    for j in range(0, cells, WIDE):
        low[:, j:j + WIDE] = full[:, j:j + WIDE].astype(jnp.bfloat16)

    def ring_rows_of(way, step, piece):
        rows_at = ring_rows(way, step)
        return pl.ds(pl.multiple_of(rows_at.start + piece * (half // CUTS), half // CUTS), half // CUTS)

    def ring_copy(way, step, piece):
        return pltpu.make_async_remote_copy(
            src_ref=part.at[ring_rows_of(way, step, piece)],
            dst_ref=ring_in.at[way, step, pl.ds(piece * (half // CUTS), half // CUTS)],
            send_sem=r_send.at[way, step, piece], recv_sem=r_recv.at[way, step, piece],
            device_id={"cell": cell_of(x, z + 1 - 2 * way + nz)}, device_id_type=MESH,
        )

    def take(way, step, target, piece):
        ring_copy(way, step, piece).wait_recv()
        at = ring_rows_of(target[0], target[1], piece)
        part[at, :] = part[at, :] + ring_in[way, step, pl.ds(piece * (half // CUTS), half // CUTS)]

    def ring_step(steps, kernels):
        acc = jnp.zeros((len(steps) * chunk, width), jnp.float32)
        for j in range(0, cells, WIDE):
            acc += times_members(kernels(j), j)
        for n, step in enumerate(steps):
            part[ring_rows(0, step), :] = acc[n * chunk:n * chunk + half]
            part[ring_rows(1, step), :] = acc[n * chunk + half:(n + 1) * chunk]
        for step in steps:
            ring_event(step)

    def ring_event(step):
        for piece in range(CUTS):
            for way in range(2):
                @pl.when(step > 1)
                def _():
                    take(way, step - 2, (way, step), piece)

                if way == 0:
                    ring_copy(0, step, piece).start()
                else:
                    ring_copy(1, step, piece).start()

    def built_step(step, carry):
        ring_step([step], lambda j: ahead[step, :, j:j + WIDE])
        return carry

    def fresh_step(i, carry):
        steps = [AHEAD[-1] + PAIR * i + n for n in range(PAIR)]
        place = [jnp.concatenate(rows, axis=0) for rows in zip(*(places(step) for step in steps))]
        ring_step(steps, lambda j: kernel_of(place, j))
        return carry

    lax.fori_loop(0, AHEAD[-1], built_step, 0)
    lax.fori_loop(0, (nz - 2 - AHEAD[-1]) // PAIR, fresh_step, 0)

    def last_step(way, carry):
        ats = [ring_rows(way, nz - 2), ring_rows(way, nz - 1)]
        place = places_at(ats)
        acc = jnp.zeros((chunk, width), jnp.float32)
        for j in range(0, cells, WIDE):
            acc += times_members(kernel_of(place, j), j)
        part[ats[0], :] = acc[:half]
        part[ats[1], :] = acc[half:]
        for piece in range(CUTS):
            for step in (nz - 2, nz - 1):
                take(way, step - 2, (way, step), piece)

                @pl.when(way == 0)
                def _():
                    ring_copy(0, step, piece).start()

        return carry

    lax.fori_loop(0, 2, last_step, 0)
    for step in (nz - 2, nz - 1):
        for piece in range(CUTS):
            take(0, step, (1, step), piece)

    x_copies = []
    for o in sorted(range(1, nx), key=lambda o: abs(o - nx // 2)):
        to = lax.rem(x + o, nx)
        x_copies.append(pltpu.make_async_remote_copy(
            src_ref=part.at[pl.ds(pl.multiple_of(z * chunk + to * final, final), final)],
            dst_ref=x_in.at[o - 1], send_sem=x_send.at[o - 1], recv_sem=x_recv.at[o - 1],
            device_id={"cell": cell_of(x + o, z)}, device_id_type=MESH,
        ))
        x_copies[-1].start()
    window = pl.ds(pl.multiple_of(z * chunk + (x // 2) * LANES, LANES), LANES)
    wide_noise[...] = jnp.broadcast_to(noise[0:1, window], (LANES, LANES)).T
    variance = wide_noise[pl.ds(pl.multiple_of(lax.rem(x, 2) * final, final), final), :]
    for c in x_copies:
        c.wait_recv()
    predicted = part[pl.ds(first, final), :]
    for o in range(nx - 1):
        predicted = predicted + x_in[o]
    predicted = predicted * (1.0 / math.sqrt(cells * nx * nz))

    anomaly = predicted - jnp.mean(predicted, axis=1, keepdims=True)
    weighted = anomaly / variance
    rows[0:width, :] = dot32(anomaly, weighted, ((0,), (0,)))
    rows[width:, :] = dot32(tgt[...] - predicted, weighted, ((0,), (0,)))

    thin = rows.shape[0] // (nx * no)
    here = x * no + obs

    def spot(piece):
        return pl.ds(pl.multiple_of(piece * thin, thin), thin)

    def other(o):
        xx, oo = lax.rem(x + o // no, nx), lax.rem(obs + lax.rem(o, no), no)
        return xx * no + oo, {"cell": xx * nz + z, "obs": oo}

    def scatter(o):
        piece, device = other(o)
        return pltpu.make_async_remote_copy(
            src_ref=rows.at[spot(piece)], dst_ref=plane_in.at[o - 1],
            send_sem=a_send.at[o - 1], recv_sem=a_recv.at[o - 1], device_id=device, device_id_type=MESH,
        )

    def along(o):
        return pltpu.make_async_remote_copy(
            src_ref=eighth, dst_ref=z_in.at[o - 1], send_sem=z_send.at[o - 1], recv_sem=z_recv.at[o - 1],
            device_id={"cell": cell_of(x, z + o)}, device_id_type=MESH,
        )

    def gather(o):
        return pltpu.make_async_remote_copy(
            src_ref=total.at[spot(here)], dst_ref=total.at[spot(here)],
            send_sem=b_send.at[o - 1], recv_sem=b_recv.at[o - 1], device_id=other(o)[1], device_id_type=MESH,
        )

    def arrived(o):
        xx, oo = lax.rem(x + nx - o // no, nx), lax.rem(obs + no - lax.rem(o, no), no)
        at = spot(xx * no + oo)
        return pltpu.make_async_remote_copy(
            src_ref=total.at[at], dst_ref=total.at[at],
            send_sem=b_send.at[o - 1], recv_sem=b_recv.at[o - 1], device_id=other(o)[1], device_id_type=MESH,
        )

    def fan(i, middle):
        return middle + ((i + 1) // 2) * (1 - 2 * lax.rem(i, 2))

    def over_plane(action):
        def one(i, carry):
            action(fan(i // no, nx // 2) * no + fan(lax.rem(i, no), no // 2))
            return carry

        lax.fori_loop(0, nx * no - 1, one, 0)

    def over_z(action):
        def one(i, carry):
            action(fan(i, nz // 2))
            return carry

        lax.fori_loop(0, nz - 1, one, 0)

    over_plane(lambda o: scatter(o).start())
    for j in range(0, cells, WIDE):
        exact = full[:, j:j + WIDE]
        rest[:, j:j + WIDE] = (exact - low[:, j:j + WIDE].astype(jnp.float32)).astype(jnp.bfloat16)
    over_plane(lambda o: scatter(o).wait_recv())
    eighth[...] = rows[spot(here), :] + jnp.sum(plane_in[...], axis=0)
    over_z(lambda o: along(o).start())
    for c in sends + x_copies:
        c.wait_send()

    def drain(step, carry):
        for piece in range(CUTS):
            ring_copy(0, step, piece).wait_send()

            @pl.when(step < nz - 2)
            def _():
                ring_copy(1, step, piece).wait_send()

        return carry

    lax.fori_loop(0, nz, drain, 0)
    over_plane(lambda o: scatter(o).wait_send())
    over_z(lambda o: along(o).wait_recv())
    total[spot(here), :] = eighth[...] + jnp.sum(z_in[...], axis=0)
    over_plane(lambda o: gather(o).start())
    over_z(lambda o: along(o).wait_send())
    over_plane(lambda o: arrived(o).wait_recv())

    mine_cross = total[pl.ds(pl.multiple_of(width + obs * mine, mine), mine), :]
    weights = solve_rows([total[i:i + SUB, :] for i in range(0, width, SUB)], mine_cross)
    weights = weights - jnp.mean(weights, axis=1, keepdims=True)
    upper = weights.astype(jnp.bfloat16)
    lower = (weights - upper.astype(jnp.float32)).astype(jnp.bfloat16)
    both = jnp.concatenate([upper, lower], axis=0)
    for j in range(0, cells, WIDE):
        main = jnp.dot(both, low[:, j:j + WIDE], preferred_element_type=jnp.float32)
        small = jnp.dot(upper, rest[:, j:j + WIDE], preferred_element_type=jnp.float32)
        out[:, j:j + WIDE] = main[:mine] + (main[mine:] + small)
    over_plane(lambda o: gather(o).wait_send())


def per_device(nx, ny, nz, station_xy, station_alt, cell_xy, cell_depth, members, targets, noise_var):
    own = members.T
    mine, cells = own.shape
    no = 2 * ny
    width = mine * no
    stations = station_alt.shape[0]
    chunk = stations // nz
    half, final = chunk // 2, chunk // nx
    thin = 2 * width // (nx * no)
    f32 = jnp.float32
    vmem = pl.BlockSpec(memory_space=pltpu.VMEM)
    dma = pltpu.SemaphoreType.DMA
    increment = pl.pallas_call(
        functools.partial(sums_kernel, nx, ny, nz),
        out_shape=jax.ShapeDtypeStruct((mine, cells), f32),
        in_specs=[pl.BlockSpec(memory_space=pltpu.HBM)] * 7,
        out_specs=vmem,
        scratch_shapes=[
            pltpu.VMEM((2, stations), f32),
            pltpu.VMEM((1, stations), f32),
            pltpu.VMEM((2, cells), f32),
            pltpu.VMEM((1, cells), f32),
            pltpu.VMEM((1, stations), f32),
            pltpu.VMEM((width, cells), f32),
            pltpu.VMEM((width, cells), jnp.bfloat16),
            pltpu.VMEM((width, cells), jnp.bfloat16),
            pltpu.VMEM((AHEAD[-1], chunk, cells), jnp.bfloat16),
            pltpu.VMEM((stations, width), f32),
            pltpu.VMEM((2, nz, half, width), f32),
            pltpu.VMEM((nx - 1, final, width), f32),
            pltpu.VMEM((final, width), f32),
            pltpu.VMEM((LANES, LANES), f32),
            pltpu.VMEM((2 * width, width), f32),
            pltpu.VMEM((nx * no - 1, thin, width), f32),
            pltpu.VMEM((thin, width), f32),
            pltpu.VMEM((nz - 1, thin, width), f32),
            pltpu.VMEM((2 * width, width), f32),
            dma((11,)), dma((11,)),
            dma((2, nz, CUTS)), dma((2, nz, CUTS)),
            dma((nx - 1,)), dma((nx - 1,)),
            dma((nx * no - 1,)), dma((nx * no - 1,)),
            dma((nz - 1,)), dma((nz - 1,)),
            dma((nx * no - 1,)), dma((nx * no - 1,)),
            dma((7,)),
        ],
        compiler_params=pltpu.CompilerParams(
            collective_id=0, has_side_effects=True, vmem_limit_bytes=64 * 2**20
        ),
    )(station_xy, station_alt[None], cell_xy, cell_depth[None], own, targets, noise_var[None])
    return increment.T


def solution(mesh):
    nz = 16
    nx = mesh.shape["cell"] // nz
    ny = mesh.shape["obs"] // 2
    placed = (
        P(None, "obs"),
        P("obs"),
        P(None, "cell"),
        P("cell"),
        P("cell", "obs"),
        P("obs", None),
        P("obs"),
    )
    return jax.shard_map(
        functools.partial(per_device, nx, ny, nz),
        mesh=mesh, in_specs=placed, out_specs=P("cell", "obs"), check_vma=False,
    )
```

```python
import functools
import math

import jax
import jax.numpy as jnp
from jax import lax
from jax.experimental import pallas as pl
from jax.experimental.pallas import tpu as pltpu
from jax.sharding import PartitionSpec as P

MESH = pl.DeviceIdType.MESH
SUB = 8
LANES = 128
WIDE = 512
AHEAD = (2, 2, 2, 2)
PAIR = 2
CUTS = 1


def dot32(a, b, dims):
    return lax.dot_general(
        a, b, (dims, ((), ())), precision=lax.Precision.HIGHEST, preferred_element_type=jnp.float32
    )


def pair_inverse(a, b, d):
    scale = 1.0 / (a * d - b * b)
    return d * scale, -b * scale, a * scale


def quad_inverse(d):
    p0, p1, p2 = pair_inverse(d[0][0], d[1][0], d[1][1])
    q = [[d[2][0], d[3][0]], [d[2][1], d[3][1]]]
    u = [[p0 * q[0][j] + p1 * q[1][j] for j in range(2)], [p1 * q[0][j] + p2 * q[1][j] for j in range(2)]]
    s = [[d[2 + i][2 + j] - (q[0][i] * u[0][j] + q[1][i] * u[1][j]) for j in range(i + 1)] for i in range(2)]
    s0, s1, s2 = pair_inverse(s[0][0], s[1][0], s[1][1])
    v = [[u[i][0] * s0 + u[i][1] * s1, u[i][0] * s1 + u[i][1] * s2] for i in range(2)]
    top = [[p0 + v[0][0] * u[0][0] + v[0][1] * u[0][1]],
           [p1 + v[1][0] * u[0][0] + v[1][1] * u[0][1], p2 + v[1][0] * u[1][0] + v[1][1] * u[1][1]]]
    return [
        [top[0][0], top[1][0], -v[0][0], -v[0][1]],
        [top[1][0], top[1][1], -v[1][0], -v[1][1]],
        [-v[0][0], -v[1][0], s0, s1],
        [-v[0][1], -v[1][1], s1, s2],
    ]


def solve_rows(gram, cross):
    width = SUB * len(gram)
    lane = lax.broadcasted_iota(jnp.int32, (SUB, LANES), 1)
    row = lax.broadcasted_iota(jnp.int32, (SUB, LANES), 0)
    tiles = [
        gram[i // SUB] + jnp.where(row + i == lane, width - 1.0, 0.0) for i in range(0, width, SUB)
    ]
    tiles += [cross[i:i + SUB] for i in range(0, cross.shape[0], SUB)]
    for k in range(0, width, 4):
        live = range((k + 4) // SUB, len(tiles))
        home, base = k // SUB, k % SUB
        pivot = tiles[home]

        def spread(tile, at):
            return jnp.broadcast_to(tile[:, at:at + 1], (SUB, LANES))

        def level(tile, at):
            return jnp.broadcast_to(tile[at:at + 1, :], (SUB, LANES))

        pivot_cols = [spread(pivot, k + j) for j in range(4)]
        block = [[level(pivot_cols[j], base + i) for j in range(i + 1)] for i in range(4)]
        inv = quad_inverse(block)
        steps = [level(pivot, base + i) for i in range(4)]
        moved = []
        for i in range(4):
            t = (inv[i][0] * steps[0] + inv[i][1] * steps[1]) + (inv[i][2] * steps[2] + inv[i][3] * steps[3])
            for m in range(4):
                t = jnp.where(lane == k + m, -inv[i][m], t)
            moved.append(t)
        for n in live:
            cols = pivot_cols if n == home else [spread(tiles[n], k + j) for j in range(4)]
            kept = jnp.where((lane >= k) & (lane < k + 4), 0.0, tiles[n])
            tiles[n] = kept - ((cols[0] * moved[0] + cols[1] * moved[1]) + (cols[2] * moved[2] + cols[3] * moved[3]))
    return jnp.concatenate(tiles[width // SUB:], axis=0)


def sums_kernel(nx, ny, nz, xy_in, alt_in, cell_xy_in, cell_dep_in, own, targets, noise_in,
                out,
                xy, alt, cell_xy, cell_dep, noise,
                full, low, rest, ahead, part, ring_in, x_in, tgt, wide_noise, rows, plane_in, eighth, z_in, total,
                g_send, g_recv, r_send, r_recv, x_send, x_recv, a_send, a_recv,
                z_send, z_recv, b_send, b_recv, local):
    obs, cell = lax.axis_index("obs"), lax.axis_index("cell")
    y, core = obs // 2, lax.rem(obs, 2)
    x, z = cell // nz, lax.rem(cell, nz)
    no = 2 * ny
    mine, cells = own.shape
    width = full.shape[0]
    stations = part.shape[0]
    chunk = stations // nz
    half = chunk // 2
    final = chunk // nx

    def obs_of(yy, cc):
        return lax.rem(yy + 2 * ny, ny) * 2 + cc

    def cell_of(xx, zz):
        return lax.rem(xx + 2 * nx, nx) * nz + lax.rem(zz + 4 * nz, nz)

    barrier = pltpu.get_barrier_semaphore()
    peers = [{"obs": o} for o in (obs_of(y, 1 - core), obs_of(y + 1, core), obs_of(y - 1, core))]
    peers += [{"cell": cell_of(x, z + 1)}, {"cell": cell_of(x, z - 1)}]
    peers += [{"cell": cell_of(x + o, z)} for o in range(1, nx)]
    for peer in peers:
        pl.semaphore_signal(barrier, inc=1, device_id=peer, device_id_type=MESH)

    mine_rows = pl.ds(pl.multiple_of(obs * mine, mine), mine)
    first = pl.multiple_of(z * chunk + x * final, final)
    loads = [
        pltpu.make_async_copy(src, dst, local.at[i]) for i, (src, dst) in enumerate((
            (own, full.at[mine_rows]), (xy_in, xy), (alt_in, alt), (cell_xy_in, cell_xy),
            (cell_dep_in, cell_dep), (noise_in, noise), (targets.at[pl.ds(first, final)], tgt),
        ))
    ]
    for c in loads:
        c.start()
    def ring_rows(way, step):
        hop = step // 2
        at = lax.rem(z + nz + nz // 2 - hop + way * (1 + 2 * hop), nz)
        return pl.ds(pl.multiple_of(at * chunk + lax.rem(step, 2) * half, half), half)

    def column(ref, row, at):
        tile = jnp.broadcast_to(ref[row:row + 1, at], (half, half)).T
        return jnp.concatenate([tile] * (WIDE // LANES), axis=1)

    def places(step):
        return places_at([ring_rows(0, step), ring_rows(1, step)])

    def places_at(ats):
        return [jnp.concatenate([column(ref, row, at) for at in ats], axis=0) for ref, row in ((xy, 0), (xy, 1), (alt, 0))]

    def kernel_of(place, j):
        dx = place[0] - cell_xy[0:1, j:j + WIDE]
        dy = place[1] - cell_xy[1:2, j:j + WIDE]
        h = place[2] + cell_dep[0:1, j:j + WIDE]
        inverse = lax.rsqrt(dx * dx + dy * dy + h * h)
        return ((h * inverse) * (inverse * inverse)).astype(jnp.bfloat16)

    def times_members(kernel, j):
        return lax.dot_general(
            kernel, low[:, j:j + WIDE], (((1,), (1,)), ((), ())), preferred_element_type=jnp.float32
        )

    cut = cells // 2
    left, right, whole = pl.ds(0, cut), pl.ds(cut, cut), pl.ds(0, cells)

    def push(block, cols, target, slot):
        at = pl.ds(pl.multiple_of(block * mine, mine), mine)
        return pltpu.make_async_remote_copy(
            src_ref=full.at[at, cols], dst_ref=full.at[at, cols],
            send_sem=g_send.at[slot], recv_sem=g_recv.at[slot],
            device_id={"obs": target}, device_id_type=MESH,
        )

    mate, up, down = obs_of(y, 1 - core), obs_of(y + 1, core), obs_of(y - 1, core)
    far = obs_of(y + 2, core)
    def push_own(cols, target, slot):
        return pltpu.make_async_remote_copy(
            src_ref=own.at[:, cols], dst_ref=full.at[mine_rows, cols],
            send_sem=g_send.at[slot], recv_sem=g_recv.at[slot],
            device_id={"obs": target}, device_id_type=MESH,
        )

    own_up = [push_own(left, up, 1), push_own(right, up, 2)]
    own_down = [push_own(right, down, 3), push_own(left, down, 4)]
    pass_up, pass_down = push(down, left, up, 5), push(up, right, down, 6)
    to_mate = [
        push_own(whole, mate, 0), push(down, whole, mate, 7), push(up, whole, mate, 8),
        push(far, left, mate, 9), push(far, right, mate, 10),
    ]
    sends = own_up + own_down + [pass_up, pass_down] + to_mate

    pl.semaphore_wait(barrier, len(peers))
    for c in (own_up[0], own_down[0], own_up[1], own_down[1], to_mate[0]):
        c.start()
    for c in loads:
        c.wait()

    def build(step, carry):
        place = places(step)
        for j in range(0, cells, WIDE):
            ahead[step, :, j:j + WIDE] = kernel_of(place, j)

        @pl.when(step == AHEAD[0] - 1)
        def _():
            push(down, left, up, 1).wait_recv()
            push(up, right, down, 3).wait_recv()
            pass_up.start()
            pass_down.start()

        @pl.when(step == AHEAD[1] - 1)
        def _():
            push(down, right, up, 2).wait_recv()
            push(up, left, down, 4).wait_recv()
            to_mate[1].start()
            to_mate[2].start()

        @pl.when(step == AHEAD[2] - 1)
        def _():
            push(far, left, up, 5).wait_recv()
            push(far, right, down, 6).wait_recv()
            to_mate[3].start()
            to_mate[4].start()

        return carry

    lax.fori_loop(0, AHEAD[-1], build, 0)
    for slot, block, cols in (
        (0, mate, whole), (7, obs_of(y - 1, 1 - core), whole), (8, obs_of(y + 1, 1 - core), whole),
        (9, obs_of(y + 2, 1 - core), left), (10, obs_of(y + 2, 1 - core), right),
    ):
        push(block, cols, mate, slot).wait_recv()
    for j in range(0, cells, WIDE):
        low[:, j:j + WIDE] = full[:, j:j + WIDE].astype(jnp.bfloat16)

    def ring_rows_of(way, step, piece):
        rows_at = ring_rows(way, step)
        return pl.ds(pl.multiple_of(rows_at.start + piece * (half // CUTS), half // CUTS), half // CUTS)

    def ring_copy(way, step, piece):
        return pltpu.make_async_remote_copy(
            src_ref=part.at[ring_rows_of(way, step, piece)],
            dst_ref=ring_in.at[way, step, pl.ds(piece * (half // CUTS), half // CUTS)],
            send_sem=r_send.at[way, step, piece], recv_sem=r_recv.at[way, step, piece],
            device_id={"cell": cell_of(x, z + 1 - 2 * way + nz)}, device_id_type=MESH,
        )

    def take(way, step, target, piece):
        ring_copy(way, step, piece).wait_recv()
        at = ring_rows_of(target[0], target[1], piece)
        part[at, :] = part[at, :] + ring_in[way, step, pl.ds(piece * (half // CUTS), half // CUTS)]

    def ring_step(steps, kernels):
        acc = jnp.zeros((len(steps) * chunk, width), jnp.float32)
        for j in range(0, cells, WIDE):
            acc += times_members(kernels(j), j)
        for n, step in enumerate(steps):
            part[ring_rows(0, step), :] = acc[n * chunk:n * chunk + half]
            part[ring_rows(1, step), :] = acc[n * chunk + half:(n + 1) * chunk]
        for step in steps:
            ring_event(step)

    def ring_event(step):
        for piece in range(CUTS):
            for way in range(2):
                @pl.when(step > 1)
                def _():
                    take(way, step - 2, (way, step), piece)

                if way == 0:
                    ring_copy(0, step, piece).start()
                else:
                    ring_copy(1, step, piece).start()

    def built_step(step, carry):
        ring_step([step], lambda j: ahead[step, :, j:j + WIDE])
        return carry

    def fresh_step(i, carry):
        steps = [AHEAD[-1] + PAIR * i + n for n in range(PAIR)]
        place = [jnp.concatenate(rows, axis=0) for rows in zip(*(places(step) for step in steps))]
        ring_step(steps, lambda j: kernel_of(place, j))
        return carry

    lax.fori_loop(0, AHEAD[-1], built_step, 0)
    lax.fori_loop(0, (nz - 2 - AHEAD[-1]) // PAIR, fresh_step, 0)

    def last_step(way, carry):
        ats = [ring_rows(way, nz - 2), ring_rows(way, nz - 1)]
        place = places_at(ats)
        acc = jnp.zeros((chunk, width), jnp.float32)
        for j in range(0, cells, WIDE):
            acc += times_members(kernel_of(place, j), j)
        part[ats[0], :] = acc[:half]
        part[ats[1], :] = acc[half:]
        for piece in range(CUTS):
            for step in (nz - 2, nz - 1):
                take(way, step - 2, (way, step), piece)

                @pl.when(way == 0)
                def _():
                    ring_copy(0, step, piece).start()

        return carry

    lax.fori_loop(0, 2, last_step, 0)
    for step in (nz - 2, nz - 1):
        for piece in range(CUTS):
            take(0, step, (1, step), piece)

    x_copies = []
    for o in sorted(range(1, nx), key=lambda o: abs(o - nx // 2)):
        to = lax.rem(x + o, nx)
        x_copies.append(pltpu.make_async_remote_copy(
            src_ref=part.at[pl.ds(pl.multiple_of(z * chunk + to * final, final), final)],
            dst_ref=x_in.at[o - 1], send_sem=x_send.at[o - 1], recv_sem=x_recv.at[o - 1],
            device_id={"cell": cell_of(x + o, z)}, device_id_type=MESH,
        ))
        x_copies[-1].start()
    window = pl.ds(pl.multiple_of(z * chunk + (x // 2) * LANES, LANES), LANES)
    wide_noise[...] = jnp.broadcast_to(noise[0:1, window], (LANES, LANES)).T
    variance = wide_noise[pl.ds(pl.multiple_of(lax.rem(x, 2) * final, final), final), :]
    for c in x_copies:
        c.wait_recv()
    predicted = part[pl.ds(first, final), :]
    for o in range(nx - 1):
        predicted = predicted + x_in[o]
    predicted = predicted * (1.0 / math.sqrt(cells * nx * nz))

    anomaly = predicted - jnp.mean(predicted, axis=1, keepdims=True)
    weighted = anomaly / variance
    rows[0:width, :] = dot32(anomaly, weighted, ((0,), (0,)))
    rows[width:, :] = dot32(tgt[...] - predicted, weighted, ((0,), (0,)))

    thin = rows.shape[0] // (nx * no)
    here = x * no + obs

    def spot(piece):
        return pl.ds(pl.multiple_of(piece * thin, thin), thin)

    def other(o):
        xx, oo = lax.rem(x + o // no, nx), lax.rem(obs + o % no, no)
        return xx * no + oo, {"cell": xx * nz + z, "obs": oo}

    def scatter(o):
        piece, device = other(o)
        return pltpu.make_async_remote_copy(
            src_ref=rows.at[spot(piece)], dst_ref=plane_in.at[o - 1],
            send_sem=a_send.at[o - 1], recv_sem=a_recv.at[o - 1], device_id=device, device_id_type=MESH,
        )

    def along(o):
        return pltpu.make_async_remote_copy(
            src_ref=eighth, dst_ref=z_in.at[o - 1], send_sem=z_send.at[o - 1], recv_sem=z_recv.at[o - 1],
            device_id={"cell": cell_of(x, z + o)}, device_id_type=MESH,
        )

    def gather(o):
        return pltpu.make_async_remote_copy(
            src_ref=total.at[spot(here)], dst_ref=total.at[spot(here)],
            send_sem=b_send.at[o - 1], recv_sem=b_recv.at[o - 1], device_id=other(o)[1], device_id_type=MESH,
        )

    def arrived(o):
        xx, oo = lax.rem(x + nx - o // no, nx), lax.rem(obs + no - o % no, no)
        at = spot(xx * no + oo)
        return pltpu.make_async_remote_copy(
            src_ref=total.at[at], dst_ref=total.at[at],
            send_sem=b_send.at[o - 1], recv_sem=b_recv.at[o - 1], device_id=other(o)[1], device_id_type=MESH,
        )

    def fan(i, middle):
        return middle + ((i + 1) // 2) * (1 - 2 * (i % 2))

    def over_plane(action):
        def one(i, carry):
            action(fan(i // no, nx // 2) * no + fan(i % no, no // 2))
            return carry

        for i in range(nx * no - 1):
            one(i, 0)

    def over_z(action):
        def one(i, carry):
            action(fan(i, nz // 2))
            return carry

        for i in range(nz - 1):
            one(i, 0)

    over_plane(lambda o: scatter(o).start())
    for j in range(0, cells, WIDE):
        exact = full[:, j:j + WIDE]
        rest[:, j:j + WIDE] = (exact - low[:, j:j + WIDE].astype(jnp.float32)).astype(jnp.bfloat16)
    over_plane(lambda o: scatter(o).wait_recv())
    eighth[...] = rows[spot(here), :] + jnp.sum(plane_in[...], axis=0)
    over_z(lambda o: along(o).start())
    for c in sends + x_copies:
        c.wait_send()

    def drain(step, carry):
        for piece in range(CUTS):
            ring_copy(0, step, piece).wait_send()

            @pl.when(step < nz - 2)
            def _():
                ring_copy(1, step, piece).wait_send()

        return carry

    lax.fori_loop(0, nz, drain, 0)
    over_plane(lambda o: scatter(o).wait_send())
    over_z(lambda o: along(o).wait_recv())
    total[spot(here), :] = eighth[...] + jnp.sum(z_in[...], axis=0)
    over_plane(lambda o: gather(o).start())
    over_z(lambda o: along(o).wait_send())
    over_plane(lambda o: arrived(o).wait_recv())

    mine_cross = total[pl.ds(pl.multiple_of(width + obs * mine, mine), mine), :]
    weights = solve_rows([total[i:i + SUB, :] for i in range(0, width, SUB)], mine_cross)
    weights = weights - jnp.mean(weights, axis=1, keepdims=True)
    upper = weights.astype(jnp.bfloat16)
    lower = (weights - upper.astype(jnp.float32)).astype(jnp.bfloat16)
    both = jnp.concatenate([upper, lower], axis=0)
    for j in range(0, cells, WIDE):
        main = jnp.dot(both, low[:, j:j + WIDE], preferred_element_type=jnp.float32)
        small = jnp.dot(upper, rest[:, j:j + WIDE], preferred_element_type=jnp.float32)
        out[:, j:j + WIDE] = main[:mine] + (main[mine:] + small)
    over_plane(lambda o: gather(o).wait_send())


def per_device(nx, ny, nz, station_xy, station_alt, cell_xy, cell_depth, members, targets, noise_var):
    own = members.T
    mine, cells = own.shape
    no = 2 * ny
    width = mine * no
    stations = station_alt.shape[0]
    chunk = stations // nz
    half, final = chunk // 2, chunk // nx
    thin = 2 * width // (nx * no)
    f32 = jnp.float32
    vmem = pl.BlockSpec(memory_space=pltpu.VMEM)
    dma = pltpu.SemaphoreType.DMA
    increment = pl.pallas_call(
        functools.partial(sums_kernel, nx, ny, nz),
        out_shape=jax.ShapeDtypeStruct((mine, cells), f32),
        in_specs=[pl.BlockSpec(memory_space=pltpu.HBM)] * 7,
        out_specs=vmem,
        scratch_shapes=[
            pltpu.VMEM((2, stations), f32),
            pltpu.VMEM((1, stations), f32),
            pltpu.VMEM((2, cells), f32),
            pltpu.VMEM((1, cells), f32),
            pltpu.VMEM((1, stations), f32),
            pltpu.VMEM((width, cells), f32),
            pltpu.VMEM((width, cells), jnp.bfloat16),
            pltpu.VMEM((width, cells), jnp.bfloat16),
            pltpu.VMEM((AHEAD[-1], chunk, cells), jnp.bfloat16),
            pltpu.VMEM((stations, width), f32),
            pltpu.VMEM((2, nz, half, width), f32),
            pltpu.VMEM((nx - 1, final, width), f32),
            pltpu.VMEM((final, width), f32),
            pltpu.VMEM((LANES, LANES), f32),
            pltpu.VMEM((2 * width, width), f32),
            pltpu.VMEM((nx * no - 1, thin, width), f32),
            pltpu.VMEM((thin, width), f32),
            pltpu.VMEM((nz - 1, thin, width), f32),
            pltpu.VMEM((2 * width, width), f32),
            dma((11,)), dma((11,)),
            dma((2, nz, CUTS)), dma((2, nz, CUTS)),
            dma((nx - 1,)), dma((nx - 1,)),
            dma((nx * no - 1,)), dma((nx * no - 1,)),
            dma((nz - 1,)), dma((nz - 1,)),
            dma((nx * no - 1,)), dma((nx * no - 1,)),
            dma((7,)),
        ],
        compiler_params=pltpu.CompilerParams(
            collective_id=0, has_side_effects=True, vmem_limit_bytes=64 * 2**20
        ),
    )(station_xy, station_alt[None], cell_xy, cell_depth[None], own, targets, noise_var[None])
    return increment.T


def solution(mesh):
    nz = 16
    nx = mesh.shape["cell"] // nz
    ny = mesh.shape["obs"] // 2
    placed = (
        P(None, "obs"),
        P("obs"),
        P(None, "cell"),
        P("cell"),
        P("cell", "obs"),
        P("obs", None),
        P("obs"),
    )
    return jax.shard_map(
        functools.partial(per_device, nx, ny, nz),
        mesh=mesh, in_specs=placed, out_specs=P("cell", "obs"), check_vma=False,
    )
```
